32 devices in a mesh: parts: 1, grid: 32 (over z, y, x, core).
Axes of the slice: x: 2, y: 2, z: 4, core: 2. Of those that a mesh axis runs over, the one named last changes fastest.
Arguments:
- tokens: bfloat16 [128, 32, 1024], P(('parts', 'grid')), may hold values from -6 to 6
- cotangent: bfloat16 [128, 32, 1024], P(('parts', 'grid')), may hold values from -6 to 6
- w_sqkv: bfloat16 [1024, 3072], P('grid'), may hold values from -0.1875 to 0.1875
- w_so: bfloat16 [1024, 1024], P('grid'), may hold values from -0.1875 to 0.1875
- w_gqkv: bfloat16 [1024, 3072], P('grid'), may hold values from -0.1875 to 0.1875
- w_go: bfloat16 [1024, 1024], P('grid'), may hold values from -0.1875 to 0.1875
- keep: int32 [32, 128], P(None, 'parts'), may hold values from 0 to 1, as said below
Outputs:
- mixed: bfloat16 [128, 32, 1024], P(('parts', 'grid'))
- token_grad: bfloat16 [128, 32, 1024], P(('parts', 'grid'))
The draws below stay inside these ranges and needn't reach their ends.
Inputs may be any that keep to these rules, and one draw needn't show every extreme that they name: `keep`: every band group keeps at least one patch; the kept share differs from group to group.
All inputs are finite; a program needn't handle non-finite values.
Results may differ from the reference program's by a relative error of at most 0.017.
Values may be sent and summed in bfloat16 or wider, within the bound.
A program may use at most 192 MiB of HBM per device.

```python
from functools import partial
import jax
import jax.numpy as jnp
from jax import lax

D = 1024
H = 16
G = 32
P_SIZE = 128


def draw_keep(key, part):
    first = jax.random.fold_in(key, 11)
    second = jax.random.fold_in(key, 12)
    cutoff = jax.random.randint(first, (G, 1), 5, 85)
    noise = jax.random.randint(second, (G, P_SIZE), 0, 100)
    kept = (noise >= cutoff).astype(jnp.int32)
    forced = (jnp.arange(P_SIZE, dtype=jnp.int32)[None, :] % G == jnp.arange(G, dtype=jnp.int32)[:, None]).astype(jnp.int32)
    return jnp.maximum(kept, forced)


def levels(key, shape, shards, smallest, largest):
    factor_of, own = 1.0, jax.random.fold_in(key, 6)
    for axis_at, blocks in shards:
        draws = jnp.exp(jax.random.uniform(jax.random.fold_in(own, axis_at), (blocks,), jnp.float32, smallest / len(shards), largest / len(shards)))
        factor_of = factor_of * jnp.repeat(draws, shape[axis_at] // blocks).reshape([-1 if axis == axis_at else 1 for axis in range(len(shape))])
    return factor_of


def scatter_about(key, extent, deviation, bound, shards=(), held_as=jnp.bfloat16):
    drawn = deviation * jax.random.normal(key, extent, jnp.float32)
    if shards:
        drawn = drawn * levels(key, extent, shards, -0.22, 0.18)
    return jnp.clip(drawn, -bound, bound).astype(held_as)


def setup_inputs(seed: int = 0, part: int = 0) -> dict:
    seeds = jax.random.split(jax.random.key(seed), 8)
    part_splits = jax.random.split(jax.random.fold_in(seeds[7], part), 8)
    tokens = scatter_about(part_splits[0], (P_SIZE, G, D), 1.0, 6.0, ((0, 32),))
    cotangent = scatter_about(part_splits[1], (P_SIZE, G, D), 1.0, 6.0, ((0, 32),))
    w_sqkv = scatter_about(seeds[2], (D, 3 * D), D ** -0.5, 0.1875, ((0, 32),))
    w_so = scatter_about(seeds[3], (D, D), D ** -0.5, 0.1875, ((0, 32),))
    w_gqkv = scatter_about(seeds[4], (D, 3 * D), D ** -0.5, 0.1875, ((0, 32),))
    w_go = scatter_about(seeds[5], (D, D), D ** -0.5, 0.1875, ((0, 32),))
    keep = draw_keep(jax.random.fold_in(jax.random.fold_in(seeds[7], part), 71), part)
    return {"tokens": tokens, "cotangent": cotangent, "w_sqkv": w_sqkv, "w_so": w_so, "w_gqkv": w_gqkv, "w_go": w_go, "keep": keep}


def rms_normalize(values):
    wide = values.astype(jnp.float32)
    meansq = lax.optimization_barrier(jnp.mean(wide * wide, axis=-1, keepdims=True))
    return (wide * lax.rsqrt(meansq + 1e-06)).astype(jnp.bfloat16)

def project_spatial(tokens, weight):
    patches, groups, width = tokens.shape
    normed = rms_normalize(tokens).reshape(patches * groups, width)
    stacked = jnp.dot(normed, weight, preferred_element_type=jnp.float32).astype(jnp.bfloat16)
    stacked = stacked.reshape(patches, groups, 3, width).transpose(2, 0, 1, 3)
    return stacked.reshape(3, patches, groups * width)

def pair_attention(operands):
    stacked, keep_row = operands
    query, keyed, valued = (stacked[0], stacked[1], stacked[2])
    scale = query.shape[-1] ** (-0.5)
    scores = jnp.dot(query, keyed.T, preferred_element_type=jnp.float32) * scale
    weights = jnp.exp(scores) * keep_row[None, :]
    probs = (weights / lax.optimization_barrier(jnp.sum(weights, axis=-1, keepdims=True))).astype(jnp.bfloat16)
    return jnp.dot(probs, valued, preferred_element_type=jnp.float32).astype(jnp.bfloat16)

def spatial_attention(stacked, keep_rows):
    three, patches, columns = stacked.shape
    pairs = keep_rows.shape[0]
    split = stacked.reshape(3, patches, pairs, columns // pairs).transpose(2, 0, 1, 3)
    result = lax.map(jax.checkpoint(pair_attention), (split, keep_rows))
    return result.transpose(1, 0, 2).reshape(patches, columns)

def block_group(tokens, attended, w_so, w_gqkv, w_go):
    patches, groups, width = tokens.shape
    rows = patches * groups
    heads = H
    y_first = (tokens.reshape(rows, width).astype(jnp.float32) + jnp.dot(attended.reshape(rows, width), w_so, preferred_element_type=jnp.float32)).astype(jnp.bfloat16)
    normed = rms_normalize(y_first)
    stacked = jnp.dot(normed, w_gqkv, preferred_element_type=jnp.float32).astype(jnp.bfloat16)
    stacked = stacked.reshape(patches, groups, 3, heads, width // heads)
    query = stacked[:, :, 0].astype(jnp.float32)
    keyed = stacked[:, :, 1].astype(jnp.float32)
    valued = stacked[:, :, 2].astype(jnp.float32)
    scale = (width // heads) ** (-0.5)
    scores = jnp.einsum('pgne,pkne->pngk', query, keyed) * scale
    weights = jnp.exp(scores)
    probs = (weights / lax.optimization_barrier(jnp.sum(weights, axis=-1, keepdims=True))).astype(jnp.bfloat16)
    result = jnp.einsum('pngk,pkne->pgne', probs.astype(jnp.float32), valued).astype(jnp.bfloat16)
    result = result.reshape(rows, width)
    mixed = (y_first.astype(jnp.float32) + jnp.dot(result, w_go, preferred_element_type=jnp.float32)).astype(jnp.bfloat16)
    return mixed.reshape(patches, groups, width)

def reference(tokens, cotangent, w_sqkv, w_so, w_gqkv, w_go, keep):
    pair_group = jnp.arange(G * H, dtype=jnp.int32) // H
    keep_rows = keep.astype(jnp.float32)[pair_group]
    stacked, pull_first = jax.vjp(partial(project_spatial, weight=w_sqkv), tokens)
    attended, pull_spatial = jax.vjp(partial(spatial_attention, keep_rows=keep_rows), stacked)
    mixed, pull_group = jax.vjp(partial(block_group, w_so=w_so, w_gqkv=w_gqkv, w_go=w_go), tokens, attended)
    grad_direct, grad_attended = pull_group(cotangent)
    grad_stacked, = pull_spatial(grad_attended)
    grad_first, = pull_first(grad_stacked)
    return (mixed, grad_direct + grad_first)
```

```python
from functools import partial

import jax
import jax.numpy as jnp
from jax import lax
from jax.experimental import pallas as pl
from jax.experimental.pallas import tpu as pltpu
from jax.sharding import PartitionSpec as P

H = 16
G = 32


def rms_normalize(values):
    wide = values.astype(jnp.float32)
    meansq = jnp.mean(wide * wide, axis=-1, keepdims=True)
    return (wide * lax.rsqrt(meansq + 1e-06)).astype(jnp.bfloat16)


def project_spatial(tokens, weight):
    patches, groups, width = tokens.shape
    normed = rms_normalize(tokens).reshape(patches * groups, width)
    stacked = jnp.dot(normed, weight, preferred_element_type=jnp.float32).astype(jnp.bfloat16)
    stacked = stacked.reshape(patches, groups, 3, width).transpose(2, 0, 1, 3)
    return stacked.reshape(3, patches, groups * width)


def pair_attention(operands):
    stacked, keep_row = operands
    query, keyed, valued = (stacked[0], stacked[1], stacked[2])
    scale = query.shape[-1] ** (-0.5)
    scores = jnp.dot(query, keyed.T, preferred_element_type=jnp.float32) * scale
    weights = jnp.exp(scores) * keep_row[None, :]
    probs = (weights / jnp.sum(weights, axis=-1, keepdims=True)).astype(jnp.bfloat16)
    return jnp.dot(probs, valued, preferred_element_type=jnp.float32).astype(jnp.bfloat16)


def spatial_attention(stacked, keep_rows, attend):
    three, patches, columns = stacked.shape
    pairs = keep_rows.shape[0]
    split = stacked.reshape(3, patches, pairs, columns // pairs).transpose(2, 0, 1, 3)
    result = lax.map(attend, (split, keep_rows))
    return result.transpose(1, 0, 2).reshape(patches, columns)


def block_group(tokens, attended, w_so, w_gqkv, w_go):
    patches, groups, width = tokens.shape
    rows = patches * groups
    heads = H
    y_first = (
        tokens.reshape(rows, width).astype(jnp.float32)
        + jnp.dot(attended.reshape(rows, width), w_so, preferred_element_type=jnp.float32)
    ).astype(jnp.bfloat16)
    normed = rms_normalize(y_first)
    stacked = jnp.dot(normed, w_gqkv, preferred_element_type=jnp.float32).astype(jnp.bfloat16)
    stacked = stacked.reshape(patches, groups, 3, heads, width // heads)
    query = stacked[:, :, 0].astype(jnp.float32)
    keyed = stacked[:, :, 1].astype(jnp.float32)
    valued = stacked[:, :, 2].astype(jnp.float32)
    scale = (width // heads) ** (-0.5)
    scores = jnp.einsum("pgne,pkne->pngk", query, keyed) * scale
    weights = jnp.exp(scores)
    probs = (weights / jnp.sum(weights, axis=-1, keepdims=True)).astype(jnp.bfloat16)
    result = jnp.einsum("pngk,pkne->pgne", probs.astype(jnp.float32), valued).astype(jnp.bfloat16)
    result = result.reshape(rows, width)
    mixed = (
        y_first.astype(jnp.float32) + jnp.dot(result, w_go, preferred_element_type=jnp.float32)
    ).astype(jnp.bfloat16)
    return mixed.reshape(patches, groups, width)


def local_any(tokens, cotangent, w_sqkv, w_so, w_gqkv, w_go, keep):
    grid_size = lax.axis_size("grid")
    position = lax.axis_index("grid")
    full_sqkv, full_so, full_gqkv, full_go = (
        lax.all_gather(w_sqkv, "grid", axis=0, tiled=True),
        lax.all_gather(w_so, "grid", axis=0, tiled=True),
        lax.all_gather(w_gqkv, "grid", axis=0, tiled=True),
        lax.all_gather(w_go, "grid", axis=0, tiled=True),
    )
    stacked, pull_first = jax.vjp(partial(project_spatial, weight=full_sqkv), tokens)
    banded = lax.all_to_all(stacked, "grid", split_axis=2, concat_axis=1, tiled=True)
    pairs = G * H // grid_size
    pair_ids = position * pairs + jnp.arange(pairs, dtype=jnp.int32)
    select = (pair_ids[:, None] // H == jnp.arange(G, dtype=jnp.int32)[None, :]).astype(jnp.float32)
    keep_rows = jnp.dot(select, keep.astype(jnp.float32), precision=lax.Precision.HIGHEST)
    attend = jax.checkpoint(pair_attention)
    attended_bands, pull_spatial = jax.vjp(
        partial(spatial_attention, keep_rows=keep_rows, attend=attend), banded
    )
    attended = lax.all_to_all(attended_bands, "grid", split_axis=0, concat_axis=1, tiled=True)
    mixed, pull_group = jax.vjp(
        partial(block_group, w_so=full_so, w_gqkv=full_gqkv, w_go=full_go), tokens, attended
    )
    grad_direct, grad_attended = pull_group(cotangent)
    grad_bands = lax.all_to_all(grad_attended, "grid", split_axis=1, concat_axis=0, tiled=True)
    (grad_banded,) = pull_spatial(grad_bands)
    grad_stacked = lax.all_to_all(grad_banded, "grid", split_axis=1, concat_axis=2, tiled=True)
    (grad_first,) = pull_first(grad_stacked)
    return (mixed, grad_direct + grad_first)

F32 = jnp.float32
BF16 = jnp.bfloat16
LANES = 128
EPS = 1e-06
TILE = 512
SPLIT = (2, 2, 2)
TRANSFERS = 93
MESH = pl.DeviceIdType.MESH


def nn(a, b):
    return lax.dot_general(a, b, (((1,), (0,)), ((), ())), preferred_element_type=F32)


def nt(a, b):
    return lax.dot_general(a, b, (((1,), (1,)), ((), ())), preferred_element_type=F32)


def tn(a, b):
    return lax.dot_general(a, b, (((0,), (0,)), ((), ())), preferred_element_type=F32)


def rms_parts(wide):
    inv = lax.rsqrt(jnp.mean(wide * wide, axis=-1, keepdims=True) + EPS)
    return inv, (wide * inv).astype(BF16)


def rms_pull(wide, inv, grad):
    inner = jnp.mean(grad * wide, axis=-1, keepdims=True)
    return grad * inv - wide * (inv * inv * inv * inner)


class Heads:
    def __init__(self, head, rows, mask):
        lane = lax.broadcasted_iota(jnp.int32, (1, LANES), 1)
        self.count = LANES // head
        self.rows = rows
        scale = head ** (-0.5)
        plain = [(lane // head == index).astype(F32) for index in range(self.count)]
        self.plain = [one.astype(BF16) for one in plain]
        self.scaled = [(one * scale).astype(BF16) for one in plain]
        self.mask = jnp.concatenate([mask] * self.count, axis=0)

    def stack(self, block, selects):
        return jnp.concatenate([block * select for select in selects], axis=0)

    def beside(self, stacked):
        rows = self.rows
        return jnp.concatenate(
            [stacked[at * rows : (at + 1) * rows] for at in range(self.count)], axis=1
        )

    def probs(self, query, keyed):
        scores = nt(self.stack(query, self.scaled), keyed)
        weights = jnp.where(self.mask, jnp.exp(scores), 0.0)
        return weights * (1.0 / jnp.sum(weights, axis=-1, keepdims=True))

    def attend(self, probs, valued):
        return nn(self.beside(probs.astype(BF16)), self.stack(valued, self.plain)).astype(BF16)

    def pull(self, probs, query, keyed, valued, grad):
        grads = self.stack(grad, self.plain)
        dprobs = nt(grads, valued).astype(BF16).astype(F32)
        inner = jnp.sum(dprobs * probs, axis=-1, keepdims=True)
        dscores = (probs * (dprobs - inner)).astype(BF16)
        dquery = nn(self.beside(dscores), self.stack(keyed, self.scaled))
        dkeyed = tn(dscores, self.stack(query, self.scaled))
        dvalued = tn(probs.astype(BF16), grads)
        return dquery.astype(BF16), dkeyed.astype(BF16), dvalued.astype(BF16)


def part_cuts(columns):
    unit = columns // 32
    return ((0, 13 * unit), (13 * unit, 26 * unit), (26 * unit, columns))


class Gather:
    def __init__(self, full_ref, rows, send_sems, recv_sems):
        self.full, self.rows = full_ref, rows
        self.send_sems, self.recv_sems = send_sems, recv_sems
        self.cuts = part_cuts(full_ref.shape[1])
        self.part, self.me = lax.axis_index("parts"), lax.axis_index("grid")
        me = self.me
        self.core, self.x, self.y, self.z = me % 2, (me // 2) % 2, (me // 4) % 2, me // 8
        z = self.z
        self.origins = (z, z + 1 - 2 * (z % 2), 2 - z // 2, 3 * (1 - z // 2))
        self.inner = (z + 1) // 2 == 1
        self.outward = self.place(z + 1 - 2 * (z % 2))
        self.inward = self.place(3 - z)
        self.xp, self.yp = self.place(z, x=1), self.place(z, y=1)
        self.cp = self.place(z, core=1)
        self.sends, self.recvs = {}, {}
        self.sent, self.sent_inner = [], []

    def place(self, z, y=0, x=0, core=0):
        ny, nx, nc = SPLIT
        y = 1 - self.y if y else self.y
        x = 1 - self.x if x else self.x
        core = 1 - self.core if core else self.core
        return ((z * ny + y) * nx + x) * nc + core

    def region(self, piece, owner):
        low, high = self.cuts[piece]
        rows = self.rows
        return self.full.at[pl.ds(pl.multiple_of(owner * rows, rows), rows), low:high]

    def copy(self, name, way, piece, owner, peer):
        at = self.sends.setdefault((name, way), len(self.sends))
        got = self.recvs.setdefault(name, len(self.recvs))
        return pltpu.make_async_remote_copy(
            src_ref=self.region(piece, owner),
            dst_ref=self.region(piece, owner),
            send_sem=self.send_sems.at[at],
            recv_sem=self.recv_sems.at[got],
            device_id=(self.part, peer),
            device_id_type=MESH,
        )

    def send(self, name, piece, owner, peer):
        made = self.copy(name, 0, piece, owner, peer)
        made.start()
        self.sent.append(made)

    def send_inner(self, name, way, piece, owner, peer):
        made = self.copy(name, way, piece, owner, peer)
        pl.when(self.inner)(made.start)
        self.sent_inner.append(made)

    def arrive(self, name, piece, owner):
        got = self.recvs.setdefault(name, len(self.recvs))
        region = self.region(piece, owner)
        pltpu.make_async_remote_copy(
            src_ref=region,
            dst_ref=region,
            send_sem=self.send_sems.at[0],
            recv_sem=self.recv_sems.at[got],
            device_id=(self.part, self.xp),
            device_id_type=MESH,
        ).wait_recv()

    def owner(self, half, j, first, second):
        cross_y, cross_x = (first, second) if half == 0 else (second, first)
        return self.place(self.origins[j], y=cross_y, x=cross_x)

    def peers(self, half):
        return (self.yp, self.xp) if half == 0 else (self.xp, self.yp)

    def z_own(self, tag, piece, owner):
        self.send((tag, 1), piece, owner, self.outward)
        self.send_inner((tag, 2), 1, piece, owner, self.inward)

    def z_pass(self, tag, piece, owner, j):
        if j == 1:
            self.send_inner((tag, 3), 1, piece, owner, self.inward)
        else:
            self.send_inner((tag, j), 2, piece, owner, self.outward)

    def spread_line(self, half, j):
        mine = self.owner(half, j, 0, 0)
        if j:
            self.arrive((("z", half), j), half, mine)
            self.z_pass(("z", half), half, mine, j)
        self.send(("first", half, j), half, mine, self.peers(half)[0])
        self.send(("second", half, j, 0), half, mine, self.peers(half)[1])
        self.send(("core", half, j, 0, 0), half, mine, self.cp)

    def spread_first(self, half, j):
        got = self.owner(half, j, 1, 0)
        self.arrive(("first", half, j), half, got)
        self.send(("second", half, j, 1), half, got, self.peers(half)[1])
        self.send(("core", half, j, 1, 0), half, got, self.cp)

    def spread_second(self, half, j, first):
        got = self.owner(half, j, first, 1)
        self.arrive(("second", half, j, first), half, got)
        self.send(("core", half, j, first, 1), half, got, self.cp)

    def flat_owner(self, j, y, x):
        return self.place(self.origins[j], y=y, x=x)

    def flat_x(self):
        got = self.flat_owner(0, 0, 1)
        self.arrive(("flat x",), 2, got)
        self.send(("flat y", 1), 2, got, self.yp)
        self.z_own(("flat z", 0, 1), 2, got)
        self.send(("flat core", 0, 0, 1), 2, got, self.cp)

    def flat_y(self, x):
        got = self.flat_owner(0, 1, x)
        self.arrive(("flat y", x), 2, got)
        self.z_own(("flat z", 1, x), 2, got)
        self.send(("flat core", 0, 1, x), 2, got, self.cp)

    def flat_z(self, j, y, x):
        got = self.flat_owner(j, y, x)
        tag = ("flat z", y, x)
        self.arrive((tag, j), 2, got)
        self.z_pass(tag, 2, got, j)
        self.send(("flat core", j, y, x), 2, got, self.cp)

    def start(self):
        me = self.me
        for half in range(2):
            self.z_own(("z", half), half, me)
        self.send(("flat x",), 2, me, self.xp)
        for half in range(2):
            self.spread_line(half, 0)
        self.send(("flat y", 0), 2, me, self.yp)
        self.z_own(("flat z", 0, 0), 2, me)
        self.send(("flat core", 0, 0, 0), 2, me, self.cp)

    def steps(self):
        halves = range(2)
        plane = [(0, 0), (0, 1), (1, 0), (1, 1)]
        work = [partial(self.flat_x)]
        work += [partial(self.spread_first, half, 0) for half in halves]
        work += [partial(self.flat_y, x) for x in range(2)]
        for j in range(1, 4):
            work += [partial(self.spread_line, half, j) for half in halves]
            work += [partial(self.spread_second, half, j - 1, 0) for half in halves]
            work += [partial(self.spread_second, half, j - 1, 1) for half in halves]
            work += [partial(self.spread_first, half, j) for half in halves]
            work += [partial(self.flat_z, j, y, x) for y, x in plane]
        work += [partial(self.spread_second, half, 3, 0) for half in halves]
        work += [partial(self.spread_second, half, 3, 1) for half in halves]
        return work

    def finish(self):
        for j in range(4):
            for first in range(2):
                for second in range(2):
                    for half in range(2):
                        cross_y, cross_x = (first, second) if half == 0 else (second, first)
                        got = self.place(self.origins[j], y=cross_y, x=cross_x, core=1)
                        self.arrive(("core", half, j, first, second), half, got)
                    got = self.place(self.origins[j], y=first, x=second, core=1)
                    self.arrive(("flat core", j, first, second), 2, got)

    def drain(self):
        for made in self.sent:
            made.wait_send()

        @pl.when(self.inner)
        def _():
            for made in self.sent_inner:
                made.wait_send()


class Exchange:
    def __init__(self, src, dst, send_sem, recv_sem):
        self.src, self.dst, self.send_sem, self.recv_sem = src, dst, send_sem, recv_sem
        self.part, self.me = lax.axis_index("parts"), lax.axis_index("grid")
        self.count = src.shape[0]

    def start(self):
        me, count = self.me, self.count

        def one(step, carry):
            peer = (me + step) % count
            pltpu.make_async_remote_copy(
                src_ref=self.src.at[peer],
                dst_ref=self.dst.at[me],
                send_sem=self.send_sem,
                recv_sem=self.recv_sem,
                device_id=(self.part, peer),
                device_id_type=MESH,
            ).start()
            return carry

        lax.fori_loop(1, count, one, 0)
        self.dst[pl.ds(me, 1)] = self.src[pl.ds(me, 1)]

    def whole(self):
        most = self.count - 1
        return pltpu.make_async_remote_copy(
            src_ref=self.src.at[0:most],
            dst_ref=self.dst.at[0:most],
            send_sem=self.send_sem,
            recv_sem=self.recv_sem,
            device_id=(self.part, (self.me + 1) % self.count),
            device_id_type=MESH,
        )

    def wait(self):
        self.whole().wait_recv()

    def drain(self):
        self.whole().wait_send()


def layer_kernel(
    head,
    tok_hbm, cot_hbm, sqkv_hbm, so_hbm, gqkv_hbm, go_hbm, keep_ref,
    mixed_ref, grad_ref,
    w_one, w_two, tok_ref, cot_ref,
    x_send, x_recv, y_send, y_recv, g_send, g_recv, h_send, h_recv,
    cot_mine, dy_ref, qkv_ref, dqkv_ref, att_ref, datt_ref, probs_ref,
    send_one, recv_one, send_two, recv_two, a2a_send, a2a_recv, own_sems,
):
    count = lax.axis_size("grid")
    part, me = lax.axis_index("parts"), lax.axis_index("grid")
    patches, groups, width = tok_ref.shape
    rows = patches * groups
    wide = 3 * width
    depth = sqkv_hbm.shape[0]
    mine = pl.ds(pl.multiple_of(me * depth, depth), depth)
    loads = [
        pltpu.make_async_copy(source, target, own_sems.at[at])
        for at, (source, target) in enumerate((
            (sqkv_hbm, w_one.at[mine, 0:wide]),
            (so_hbm, w_one.at[mine, wide : wide + width]),
            (gqkv_hbm, w_two.at[mine, 0:wide]),
            (go_hbm, w_two.at[mine, wide : wide + width]),
            (tok_hbm, tok_ref),
            (cot_hbm, cot_ref),
        ))
    ]
    for load in loads:
        load.start()

    barrier = pltpu.get_barrier_semaphore()

    def greet(step, carry):
        pl.semaphore_signal(
            barrier, inc=1, device_id=(part, (me + step) % count), device_id_type=MESH
        )
        return carry

    lax.fori_loop(1, count, greet, 0)
    loads[4].wait()
    for at in range(patches):
        x_send[:, at, :] = tok_ref[at]
    for load in loads[:4]:
        load.wait()
    pl.semaphore_wait(barrier, count - 1)

    one = Gather(w_one, depth, send_one, recv_one)
    two = Gather(w_two, depth, send_two, recv_two)
    bands = Exchange(x_send, x_recv, a2a_send.at[0], a2a_recv.at[0])
    back = Exchange(y_send, y_recv, a2a_send.at[1], a2a_recv.at[1])
    pull = Exchange(g_send, g_recv, a2a_send.at[2], a2a_recv.at[2])
    home = Exchange(h_send, h_recv, a2a_send.at[3], a2a_recv.at[3])

    one.start()
    bands.start()
    loads[5].wait()
    for at in range(patches):
        cot_mine[:, at, :] = cot_ref[at]
    for step in one.steps():
        step()
    two.start()
    ahead = two.steps()

    def pump(steps):
        for _ in range(min(steps, len(ahead))):
            ahead.pop(0)()

    one.finish()
    bands.wait()

    def part_at(ref, piece, at):
        return ref[:, piece * width + at : piece * width + at + LANES]

    x = x_recv[...].reshape(rows, width).astype(F32)
    _, normed = rms_parts(x)
    for at in range(0, wide, TILE):
        qkv_ref[:, at : at + TILE] = nn(normed, w_one[:, at : at + TILE]).astype(BF16)
    pump(1)
    keep_row = keep_ref[pl.ds(me, 1), :]
    space = Heads(head, rows, jnp.broadcast_to(keep_row, (rows, rows)) > 0)
    stacked = space.count * rows
    for block in range(width // LANES):
        at = block * LANES
        query, keyed, valued = (part_at(qkv_ref, piece, at) for piece in range(3))
        probs = space.probs(query, keyed)
        probs_ref[block * stacked : (block + 1) * stacked, :] = probs
        att_ref[:, at : at + LANES] = space.attend(probs, valued)
        pump(1)
    attended = att_ref[...]
    for at in range(0, width, TILE):
        y = x[:, at : at + TILE] + nn(attended, w_one[:, wide + at : wide + at + TILE])
        y_send[:, :, at : at + TILE] = y.astype(BF16).reshape(groups, patches, TILE)
    back.start()
    pump(len(ahead))
    two.finish()

    cot = cot_mine[...].reshape(rows, width)
    for at in range(0, width, TILE):
        datt_ref[:, at : at + TILE] = nt(cot, w_two[wide_rows(at), wide : wide + width]).astype(BF16)
    back.wait()
    y_first = y_recv[...].reshape(rows, width).astype(F32)
    inv, normed = rms_parts(y_first)
    for at in range(0, wide, TILE):
        dqkv_ref[:, at : at + TILE] = nn(normed, w_two[:, at : at + TILE]).astype(BF16)
    row = lax.broadcasted_iota(jnp.int32, (rows, rows), 0)
    col = lax.broadcasted_iota(jnp.int32, (rows, rows), 1)
    across = Heads(head, rows, row % patches == col % patches)
    for block in range(width // LANES):
        at = block * LANES
        query, keyed, valued = (part_at(dqkv_ref, piece, at) for piece in range(3))
        grad = datt_ref[:, at : at + LANES]
        probs = across.probs(query, keyed)
        att_ref[:, at : at + LANES] = across.attend(probs, valued)
        for piece, pulled in enumerate(across.pull(probs, query, keyed, valued, grad)):
            dqkv_ref[:, piece * width + at : piece * width + at + LANES] = pulled
    for at in range(0, width, TILE):
        datt_ref[:, at : at + TILE] = nt(dqkv_ref[...], w_two[wide_rows(at), 0:wide]).astype(BF16)
    dy = cot + rms_pull(y_first, inv, datt_ref[...].astype(F32)).astype(BF16)
    dy_ref[...] = dy
    for at in range(0, width, TILE):
        back_grad = nt(dy, w_one[wide_rows(at), wide : wide + width]).astype(BF16)
        g_send[:, :, at : at + TILE] = back_grad.reshape(groups, patches, TILE)
    pull.start()
    attended = att_ref[...]
    for at in range(0, width, TILE):
        out = y_first[:, at : at + TILE] + nn(attended, w_two[:, wide + at : wide + at + TILE])
        mixed_ref[:, :, at : at + TILE] = out.astype(BF16).reshape(groups, patches, TILE)
    pull.wait()

    datt_ref[...] = g_recv[...].reshape(rows, width)
    for block in range(width // LANES):
        at = block * LANES
        query, keyed, valued = (part_at(qkv_ref, piece, at) for piece in range(3))
        probs = probs_ref[block * stacked : (block + 1) * stacked, :]
        grad = datt_ref[:, at : at + LANES]
        for piece, pulled in enumerate(space.pull(probs, query, keyed, valued, grad)):
            dqkv_ref[:, piece * width + at : piece * width + at + LANES] = pulled
    for at in range(0, width, TILE):
        grad = nt(dqkv_ref[...], w_one[wide_rows(at), 0:wide]).astype(BF16)
        h_send[:, :, at : at + TILE] = grad.reshape(groups, patches, TILE)
    home.start()
    own = x_send[...].reshape(rows, width).astype(F32)
    inv, _ = rms_parts(own)
    for gather in (one, two):
        gather.drain()
    home.wait()
    first = rms_pull(own, inv, h_recv[...].reshape(rows, width).astype(F32)).astype(BF16)
    grad_ref[...] = (dy_ref[...] + first).reshape(groups, patches, width)
    for exchange in (bands, back, pull, home):
        exchange.drain()


def wide_rows(at):
    return slice(at, at + TILE)


def local_bands(tokens, cotangent, w_sqkv, w_so, w_gqkv, w_go, keep):
    patches, groups, width = tokens.shape
    rows = patches * groups
    head = width // H
    count = lax.axis_size("grid")
    depth = w_sqkv.shape[0]
    banded = (groups, patches, width)
    flat, wide = (rows, width), (rows, 3 * width)
    full = (depth * count, 4 * width)
    shapes = [full, full, tokens.shape, tokens.shape]
    shapes += [banded] * 8
    shapes += [banded, flat, wide, wide, flat, flat]
    anywhere = pl.BlockSpec(memory_space=pl.ANY)
    vmem = pl.BlockSpec(memory_space=pltpu.VMEM)
    product = 2 * rows * width * width
    mixed, grad = pl.pallas_call(
        partial(layer_kernel, head),
        in_specs=[anywhere] * 6 + [vmem],
        out_specs=(vmem, vmem),
        out_shape=(jax.ShapeDtypeStruct(banded, BF16),) * 2,
        scratch_shapes=[pltpu.VMEM(shape, BF16) for shape in shapes]
        + [pltpu.VMEM((H * rows, rows), F32)]
        + [pltpu.SemaphoreType.DMA((TRANSFERS + 32,)), pltpu.SemaphoreType.DMA((TRANSFERS,))] * 2
        + [pltpu.SemaphoreType.DMA((4,)), pltpu.SemaphoreType.DMA((4,)), pltpu.SemaphoreType.DMA((6,))],
        compiler_params=pltpu.CompilerParams(
            collective_id=0, has_side_effects=True, vmem_limit_bytes=40 * 2**20
        ),
        cost_estimate=pl.CostEstimate(
            flops=21 * product, bytes_accessed=2**20, transcendentals=0
        ),
    )(tokens, cotangent, w_sqkv, w_so, w_gqkv, w_go, keep)
    return mixed.transpose(1, 0, 2), grad.transpose(1, 0, 2)


def local(tokens, *rest):
    if lax.axis_size("grid") == tokens.shape[1]:
        return local_bands(tokens, *rest)
    return local_any(tokens, *rest)


def solution(mesh):
    placed = (
        P(("parts", "grid"), None, None),
        P(("parts", "grid"), None, None),
        P("grid", None),
        P("grid", None),
        P("grid", None),
        P("grid", None),
        P(None, "parts"),
    )
    return jax.shard_map(
        local,
        mesh=mesh,
        in_specs=placed,
        out_specs=(P(("parts", "grid"), None, None), P(("parts", "grid"), None, None)),
        check_vma=False,
    )
```

```python
from functools import partial

import jax
import jax.numpy as jnp
from jax import lax
from jax.experimental import pallas as pl
from jax.experimental.pallas import tpu as pltpu
from jax.sharding import PartitionSpec as P

H = 16
G = 32


def rms_normalize(values):
    wide = values.astype(jnp.float32)
    meansq = jnp.mean(wide * wide, axis=-1, keepdims=True)
    return (wide * lax.rsqrt(meansq + 1e-06)).astype(jnp.bfloat16)


def project_spatial(tokens, weight):
    patches, groups, width = tokens.shape
    normed = rms_normalize(tokens).reshape(patches * groups, width)
    stacked = jnp.dot(normed, weight, preferred_element_type=jnp.float32).astype(jnp.bfloat16)
    stacked = stacked.reshape(patches, groups, 3, width).transpose(2, 0, 1, 3)
    return stacked.reshape(3, patches, groups * width)


def pair_attention(operands):
    stacked, keep_row = operands
    query, keyed, valued = (stacked[0], stacked[1], stacked[2])
    scale = query.shape[-1] ** (-0.5)
    scores = jnp.dot(query, keyed.T, preferred_element_type=jnp.float32) * scale
    weights = jnp.exp(scores) * keep_row[None, :]
    probs = (weights / jnp.sum(weights, axis=-1, keepdims=True)).astype(jnp.bfloat16)
    return jnp.dot(probs, valued, preferred_element_type=jnp.float32).astype(jnp.bfloat16)


def spatial_attention(stacked, keep_rows, attend):
    three, patches, columns = stacked.shape
    pairs = keep_rows.shape[0]
    split = stacked.reshape(3, patches, pairs, columns // pairs).transpose(2, 0, 1, 3)
    result = lax.map(attend, (split, keep_rows))
    return result.transpose(1, 0, 2).reshape(patches, columns)


def block_group(tokens, attended, w_so, w_gqkv, w_go):
    patches, groups, width = tokens.shape
    rows = patches * groups
    heads = H
    y_first = (
        tokens.reshape(rows, width).astype(jnp.float32)
        + jnp.dot(attended.reshape(rows, width), w_so, preferred_element_type=jnp.float32)
    ).astype(jnp.bfloat16)
    normed = rms_normalize(y_first)
    stacked = jnp.dot(normed, w_gqkv, preferred_element_type=jnp.float32).astype(jnp.bfloat16)
    stacked = stacked.reshape(patches, groups, 3, heads, width // heads)
    query = stacked[:, :, 0].astype(jnp.float32)
    keyed = stacked[:, :, 1].astype(jnp.float32)
    valued = stacked[:, :, 2].astype(jnp.float32)
    scale = (width // heads) ** (-0.5)
    scores = jnp.einsum("pgne,pkne->pngk", query, keyed) * scale
    weights = jnp.exp(scores)
    probs = (weights / jnp.sum(weights, axis=-1, keepdims=True)).astype(jnp.bfloat16)
    result = jnp.einsum("pngk,pkne->pgne", probs.astype(jnp.float32), valued).astype(jnp.bfloat16)
    result = result.reshape(rows, width)
    mixed = (
        y_first.astype(jnp.float32) + jnp.dot(result, w_go, preferred_element_type=jnp.float32)
    ).astype(jnp.bfloat16)
    return mixed.reshape(patches, groups, width)


def local_any(tokens, cotangent, w_sqkv, w_so, w_gqkv, w_go, keep):
    grid_size = lax.axis_size("grid")
    position = lax.axis_index("grid")
    full_sqkv, full_so, full_gqkv, full_go = (
        lax.all_gather(w_sqkv, "grid", axis=0, tiled=True),
        lax.all_gather(w_so, "grid", axis=0, tiled=True),
        lax.all_gather(w_gqkv, "grid", axis=0, tiled=True),
        lax.all_gather(w_go, "grid", axis=0, tiled=True),
    )
    stacked, pull_first = jax.vjp(partial(project_spatial, weight=full_sqkv), tokens)
    banded = lax.all_to_all(stacked, "grid", split_axis=2, concat_axis=1, tiled=True)
    pairs = G * H // grid_size
    pair_ids = position * pairs + jnp.arange(pairs, dtype=jnp.int32)
    select = (pair_ids[:, None] // H == jnp.arange(G, dtype=jnp.int32)[None, :]).astype(jnp.float32)
    keep_rows = jnp.dot(select, keep.astype(jnp.float32), precision=lax.Precision.HIGHEST)
    attend = jax.checkpoint(pair_attention)
    attended_bands, pull_spatial = jax.vjp(
        partial(spatial_attention, keep_rows=keep_rows, attend=attend), banded
    )
    attended = lax.all_to_all(attended_bands, "grid", split_axis=0, concat_axis=1, tiled=True)
    mixed, pull_group = jax.vjp(
        partial(block_group, w_so=full_so, w_gqkv=full_gqkv, w_go=full_go), tokens, attended
    )
    grad_direct, grad_attended = pull_group(cotangent)
    grad_bands = lax.all_to_all(grad_attended, "grid", split_axis=1, concat_axis=0, tiled=True)
    (grad_banded,) = pull_spatial(grad_bands)
    grad_stacked = lax.all_to_all(grad_banded, "grid", split_axis=1, concat_axis=2, tiled=True)
    (grad_first,) = pull_first(grad_stacked)
    return (mixed, grad_direct + grad_first)

F32 = jnp.float32
BF16 = jnp.bfloat16
LANES = 128
EPS = 1e-06
TILE = 512
SPLIT = (2, 2, 2)
TRANSFERS = 93
LAG = 12
MESH = pl.DeviceIdType.MESH


def nn(a, b):
    return lax.dot_general(a, b, (((1,), (0,)), ((), ())), preferred_element_type=F32)


def nt(a, b):
    return lax.dot_general(a, b, (((1,), (1,)), ((), ())), preferred_element_type=F32)


def tn(a, b):
    return lax.dot_general(a, b, (((0,), (0,)), ((), ())), preferred_element_type=F32)


def rms_parts(wide):
    inv = lax.rsqrt(jnp.mean(wide * wide, axis=-1, keepdims=True) + EPS)
    return inv, (wide * inv).astype(BF16)


def rms_pull(wide, inv, grad):
    inner = jnp.mean(grad * wide, axis=-1, keepdims=True)
    return grad * inv - wide * (inv * inv * inv * inner)


class Heads:
    def __init__(self, head, rows, mask):
        lane = lax.broadcasted_iota(jnp.int32, (1, LANES), 1)
        self.count = LANES // head
        self.rows = rows
        scale = head ** (-0.5)
        plain = [(lane // head == index).astype(F32) for index in range(self.count)]
        self.plain = [one.astype(BF16) for one in plain]
        self.scaled = [(one * scale).astype(BF16) for one in plain]
        self.mask = jnp.concatenate([mask] * self.count, axis=0)

    def stack(self, block, selects):
        return jnp.concatenate([block * select for select in selects], axis=0)

    def beside(self, stacked):
        rows = self.rows
        return jnp.concatenate(
            [stacked[at * rows : (at + 1) * rows] for at in range(self.count)], axis=1
        )

    def probs(self, query, keyed):
        scores = nt(self.stack(query, self.scaled), keyed)
        weights = jnp.where(self.mask, jnp.exp(scores), 0.0)
        return weights * (1.0 / jnp.sum(weights, axis=-1, keepdims=True))

    def attend(self, probs, valued):
        return nn(self.beside(probs.astype(BF16)), self.stack(valued, self.plain)).astype(BF16)

    def pull(self, probs, query, keyed, valued, grad):
        grads = self.stack(grad, self.plain)
        dprobs = nt(grads, valued).astype(BF16).astype(F32)
        inner = jnp.sum(dprobs * probs, axis=-1, keepdims=True)
        dscores = (probs * (dprobs - inner)).astype(BF16)
        dquery = nn(self.beside(dscores), self.stack(keyed, self.scaled))
        dkeyed = tn(dscores, self.stack(query, self.scaled))
        dvalued = tn(probs.astype(BF16), grads)
        return dquery.astype(BF16), dkeyed.astype(BF16), dvalued.astype(BF16)


def part_cuts(columns):
    unit = columns // 32
    return ((0, 13 * unit), (13 * unit, 26 * unit), (26 * unit, columns))


class Gather:
    def __init__(self, full_ref, rows, send_sems, recv_sems):
        self.full, self.rows = full_ref, rows
        self.send_sems, self.recv_sems = send_sems, recv_sems
        self.cuts = part_cuts(full_ref.shape[1])
        self.part, self.me = lax.axis_index("parts"), lax.axis_index("grid")
        me = self.me
        self.core, self.x, self.y, self.z = me % 2, (me // 2) % 2, (me // 4) % 2, me // 8
        z = self.z
        self.origins = (z, z + 1 - 2 * (z % 2), 2 - z // 2, 3 * (1 - z // 2))
        self.inner = (z + 1) // 2 == 1
        self.outward = self.place(z + 1 - 2 * (z % 2))
        self.inward = self.place(3 - z)
        self.xp, self.yp = self.place(z, x=1), self.place(z, y=1)
        self.cp = self.place(z, core=1)
        self.sends, self.recvs = {}, {}
        self.sent, self.sent_inner = [], []

    def place(self, z, y=0, x=0, core=0):
        ny, nx, nc = SPLIT
        y = 1 - self.y if y else self.y
        x = 1 - self.x if x else self.x
        core = 1 - self.core if core else self.core
        return ((z * ny + y) * nx + x) * nc + core

    def region(self, piece, owner):
        low, high = self.cuts[piece]
        rows = self.rows
        return self.full.at[pl.ds(pl.multiple_of(owner * rows, rows), rows), low:high]

    def copy(self, name, way, piece, owner, peer):
        at = self.sends.setdefault((name, way), len(self.sends))
        got = self.recvs.setdefault(name, len(self.recvs))
        return pltpu.make_async_remote_copy(
            src_ref=self.region(piece, owner),
            dst_ref=self.region(piece, owner),
            send_sem=self.send_sems.at[at],
            recv_sem=self.recv_sems.at[got],
            device_id=(self.part, peer),
            device_id_type=MESH,
        )

    def send(self, name, piece, owner, peer):
        made = self.copy(name, 0, piece, owner, peer)
        made.start()
        self.sent.append(made)

    def send_inner(self, name, way, piece, owner, peer):
        made = self.copy(name, way, piece, owner, peer)
        pl.when(self.inner)(made.start)
        self.sent_inner.append(made)

    def arrive(self, name, piece, owner):
        got = self.recvs.setdefault(name, len(self.recvs))
        region = self.region(piece, owner)
        pltpu.make_async_remote_copy(
            src_ref=region,
            dst_ref=region,
            send_sem=self.send_sems.at[0],
            recv_sem=self.recv_sems.at[got],
            device_id=(self.part, self.xp),
            device_id_type=MESH,
        ).wait_recv()

    def owner(self, half, j, first, second):
        cross_y, cross_x = (first, second) if half == 0 else (second, first)
        return self.place(self.origins[j], y=cross_y, x=cross_x)

    def peers(self, half):
        return (self.yp, self.xp) if half == 0 else (self.xp, self.yp)

    def z_own(self, tag, piece, owner):
        self.send((tag, 1), piece, owner, self.outward)
        self.send_inner((tag, 2), 1, piece, owner, self.inward)

    def z_pass(self, tag, piece, owner, j):
        if j == 1:
            self.send_inner((tag, 3), 1, piece, owner, self.inward)
        else:
            self.send_inner((tag, j), 2, piece, owner, self.outward)

    def spread_line(self, half, j):
        mine = self.owner(half, j, 0, 0)
        if j:
            self.arrive((("z", half), j), half, mine)
            self.z_pass(("z", half), half, mine, j)
        self.send(("first", half, j), half, mine, self.peers(half)[0])
        self.send(("second", half, j, 0), half, mine, self.peers(half)[1])
        self.send(("core", half, j, 0, 0), half, mine, self.cp)

    def spread_first(self, half, j):
        got = self.owner(half, j, 1, 0)
        self.arrive(("first", half, j), half, got)
        self.send(("second", half, j, 1), half, got, self.peers(half)[1])
        self.send(("core", half, j, 1, 0), half, got, self.cp)

    def spread_second(self, half, j, first):
        got = self.owner(half, j, first, 1)
        self.arrive(("second", half, j, first), half, got)
        self.send(("core", half, j, first, 1), half, got, self.cp)

    def flat_owner(self, j, y, x):
        return self.place(self.origins[j], y=y, x=x)

    def flat_x(self):
        got = self.flat_owner(0, 0, 1)
        self.arrive(("flat x",), 2, got)
        self.send(("flat y", 1), 2, got, self.yp)
        self.z_own(("flat z", 0, 1), 2, got)
        self.send(("flat core", 0, 0, 1), 2, got, self.cp)

    def flat_y(self, x):
        got = self.flat_owner(0, 1, x)
        self.arrive(("flat y", x), 2, got)
        self.z_own(("flat z", 1, x), 2, got)
        self.send(("flat core", 0, 1, x), 2, got, self.cp)

    def flat_z(self, j, y, x):
        got = self.flat_owner(j, y, x)
        tag = ("flat z", y, x)
        self.arrive((tag, j), 2, got)
        self.z_pass(tag, 2, got, j)
        self.send(("flat core", j, y, x), 2, got, self.cp)

    def start(self):
        me = self.me
        for half in range(2):
            self.z_own(("z", half), half, me)
        self.send(("flat x",), 2, me, self.xp)
        for half in range(2):
            self.spread_line(half, 0)
        self.send(("flat y", 0), 2, me, self.yp)
        self.z_own(("flat z", 0, 0), 2, me)
        self.send(("flat core", 0, 0, 0), 2, me, self.cp)

    def steps(self):
        halves = range(2)
        plane = [(0, 0), (0, 1), (1, 0), (1, 1)]
        work = [partial(self.flat_x)]
        work += [partial(self.spread_first, half, 0) for half in halves]
        work += [partial(self.flat_y, x) for x in range(2)]
        for j in range(1, 4):
            work += [partial(self.spread_line, half, j) for half in halves]
            work += [partial(self.spread_second, half, j - 1, 0) for half in halves]
            work += [partial(self.spread_second, half, j - 1, 1) for half in halves]
            work += [partial(self.spread_first, half, j) for half in halves]
            work += [partial(self.flat_z, j, y, x) for y, x in plane]
        work += [partial(self.spread_second, half, 3, 0) for half in halves]
        work += [partial(self.spread_second, half, 3, 1) for half in halves]
        return work

    def finish(self):
        for j in range(4):
            for first in range(2):
                for second in range(2):
                    for half in range(2):
                        cross_y, cross_x = (first, second) if half == 0 else (second, first)
                        got = self.place(self.origins[j], y=cross_y, x=cross_x, core=1)
                        self.arrive(("core", half, j, first, second), half, got)
                    got = self.place(self.origins[j], y=first, x=second, core=1)
                    self.arrive(("flat core", j, first, second), 2, got)

    def drain(self):
        for made in self.sent:
            made.wait_send()

        @pl.when(self.inner)
        def _():
            for made in self.sent_inner:
                made.wait_send()


class Exchange:
    def __init__(self, src, dst, send_sems, recv_sems, tiles=1):
        self.src, self.dst, self.send_sems, self.recv_sems = src, dst, send_sems, recv_sems
        self.part, self.me = lax.axis_index("parts"), lax.axis_index("grid")
        self.count, self.tiles = src.shape[0], tiles
        self.wide = src.shape[2] // tiles

    def columns(self, tile):
        return slice(tile * self.wide, (tile + 1) * self.wide)

    def start(self, tile=0):
        me, count, columns = self.me, self.count, self.columns(tile)

        def one(step, carry):
            peer = (me + step) % count
            pltpu.make_async_remote_copy(
                src_ref=self.src.at[peer, :, columns],
                dst_ref=self.dst.at[me, :, columns],
                send_sem=self.send_sems.at[tile],
                recv_sem=self.recv_sems.at[tile],
                device_id=(self.part, peer),
                device_id_type=MESH,
            ).start()
            return carry

        lax.fori_loop(1, count, one, 0)
        self.dst[pl.ds(me, 1), :, columns] = self.src[pl.ds(me, 1), :, columns]

    def whole(self, tile):
        most, columns = self.count - 1, self.columns(tile)
        return pltpu.make_async_remote_copy(
            src_ref=self.src.at[0:most, :, columns],
            dst_ref=self.dst.at[0:most, :, columns],
            send_sem=self.send_sems.at[tile],
            recv_sem=self.recv_sems.at[tile],
            device_id=(self.part, (self.me + 1) % self.count),
            device_id_type=MESH,
        )

    def wait(self, tile=0):
        self.whole(tile).wait_recv()

    def drain(self):
        for tile in range(self.tiles):
            self.whole(tile).wait_send()


class Greeting:
    def __init__(self, gather, sems):
        self.at, self.sems = gather, sems

    def signal(self, sem, peer):
        pl.semaphore_signal(
            sem, inc=1, device_id=(self.at.part, peer), device_id_type=MESH
        )

    def neighbours(self):
        at, barrier = self.at, pltpu.get_barrier_semaphore()
        for peer in (at.xp, at.yp, at.cp, at.outward):
            self.signal(barrier, peer)

        @pl.when(at.inner)
        def _():
            self.signal(barrier, at.inward)

    def meet(self):
        at, barrier = self.at, pltpu.get_barrier_semaphore()
        pl.semaphore_wait(barrier, 4 + jnp.where(at.inner, 1, 0))
        self.signal(self.sems.at[0], at.cp)

    def stages(self):
        at, sems = self.at, self.sems
        order = (at.cp, at.xp, at.yp, at.outward)

        def pass_on(stage):
            pl.semaphore_wait(sems.at[stage], 1)
            self.signal(sems.at[stage + 1], order[stage + 1])

        def across():
            pl.semaphore_wait(sems.at[3], 1)

            @pl.when(at.inner)
            def _():
                self.signal(sems.at[4], at.inward)

        def ends():
            @pl.when(at.inner)
            def _():
                pl.semaphore_wait(sems.at[4], 1)
                self.signal(sems.at[5], at.outward)

            @pl.when(jnp.logical_not(at.inner))
            def _():
                pl.semaphore_wait(sems.at[5], 1)

        return [partial(pass_on, stage) for stage in range(3)] + [across, ends]


def layer_kernel(
    head,
    tok_hbm, cot_hbm, sqkv_hbm, so_hbm, gqkv_hbm, go_hbm, keep_ref,
    mixed_ref, grad_ref,
    w_one, w_two, tok_ref, cot_ref,
    x_send, x_recv, y_send, y_recv, g_send, g_recv, h_send, h_recv,
    cot_mine, dy_ref, qkv_ref, dqkv_ref, att_ref, datt_ref, probs_ref,
    send_one, recv_one, send_two, recv_two, a2a_send, a2a_recv, own_sems, hello,
):
    count = lax.axis_size("grid")
    part, me = lax.axis_index("parts"), lax.axis_index("grid")
    patches, groups, width = tok_ref.shape
    rows = patches * groups
    wide = 3 * width
    depth = sqkv_hbm.shape[0]
    mine = pl.ds(pl.multiple_of(me * depth, depth), depth)
    loads = [
        pltpu.make_async_copy(source, target, own_sems.at[at])
        for at, (source, target) in enumerate((
            (sqkv_hbm, w_one.at[mine, 0:wide]),
            (so_hbm, w_one.at[mine, wide : wide + width]),
            (gqkv_hbm, w_two.at[mine, 0:wide]),
            (go_hbm, w_two.at[mine, wide : wide + width]),
            (tok_hbm, tok_ref),
            (cot_hbm, cot_ref),
        ))
    ]
    for load in loads:
        load.start()

    one = Gather(w_one, depth, send_one, recv_one)
    two = Gather(w_two, depth, send_two, recv_two)
    greeting = Greeting(one, hello)
    bands = Exchange(x_send, x_recv, a2a_send.at[0], a2a_recv.at[0])
    back = Exchange(y_send, y_recv, a2a_send.at[1], a2a_recv.at[1])
    pull = Exchange(g_send, g_recv, a2a_send.at[2], a2a_recv.at[2], width // TILE)
    home = Exchange(h_send, h_recv, a2a_send.at[3], a2a_recv.at[3], width // TILE)

    greeting.neighbours()
    for load in loads[:4]:
        load.wait()
    greeting.meet()
    one.start()
    loads[4].wait()
    for at in range(patches):
        x_send[:, at, :] = tok_ref[at]
    loads[5].wait()
    for at in range(patches):
        cot_mine[:, at, :] = cot_ref[at]
    stages = greeting.stages()
    ahead = two.steps()

    def pump(steps):
        for _ in range(min(steps, len(ahead))):
            ahead.pop(0)()

    for at, step in enumerate(one.steps()):
        if at < len(stages):
            stages[at]()
        step()
        if at == len(stages):
            bands.start()
        if at == LAG:
            two.start()
        if at > LAG:
            pump(1)
    one.finish()
    bands.wait()

    def part_at(ref, piece, at):
        return ref[:, piece * width + at : piece * width + at + LANES]

    x = x_recv[...].reshape(rows, width).astype(F32)
    _, normed = rms_parts(x)
    for at in range(0, wide, TILE):
        qkv_ref[:, at : at + TILE] = nn(normed, w_one[:, at : at + TILE]).astype(BF16)
    pump(1)
    keep_row = keep_ref[pl.ds(me, 1), :]
    space = Heads(head, rows, jnp.broadcast_to(keep_row, (rows, rows)) > 0)
    stacked = space.count * rows
    for block in range(width // LANES):
        at = block * LANES
        query, keyed, valued = (part_at(qkv_ref, piece, at) for piece in range(3))
        probs = space.probs(query, keyed)
        probs_ref[block * stacked : (block + 1) * stacked, :] = probs
        att_ref[:, at : at + LANES] = space.attend(probs, valued)
        pump(1)
    attended = att_ref[...]
    for at in range(0, width, TILE):
        y = x[:, at : at + TILE] + nn(attended, w_one[:, wide + at : wide + at + TILE])
        y_send[:, :, at : at + TILE] = y.astype(BF16).reshape(groups, patches, TILE)
    back.start()
    pump(len(ahead))
    two.finish()

    cot = cot_mine[...].reshape(rows, width)
    for at in range(0, width, TILE):
        datt_ref[:, at : at + TILE] = nt(cot, w_two[wide_rows(at), wide : wide + width]).astype(BF16)
    back.wait()
    y_first = y_recv[...].reshape(rows, width).astype(F32)
    inv, normed = rms_parts(y_first)
    for at in range(0, wide, TILE):
        dqkv_ref[:, at : at + TILE] = nn(normed, w_two[:, at : at + TILE]).astype(BF16)
    row = lax.broadcasted_iota(jnp.int32, (rows, rows), 0)
    col = lax.broadcasted_iota(jnp.int32, (rows, rows), 1)
    across = Heads(head, rows, row % patches == col % patches)
    for block in range(width // LANES):
        at = block * LANES
        query, keyed, valued = (part_at(dqkv_ref, piece, at) for piece in range(3))
        grad = datt_ref[:, at : at + LANES]
        probs = across.probs(query, keyed)
        att_ref[:, at : at + LANES] = across.attend(probs, valued)
        for piece, pulled in enumerate(across.pull(probs, query, keyed, valued, grad)):
            dqkv_ref[:, piece * width + at : piece * width + at + LANES] = pulled
    for at in range(0, width, TILE):
        datt_ref[:, at : at + TILE] = nt(dqkv_ref[...], w_two[wide_rows(at), 0:wide]).astype(BF16)
    dy = cot + rms_pull(y_first, inv, datt_ref[...].astype(F32)).astype(BF16)
    dy_ref[...] = dy
    for at in range(0, width, TILE):
        back_grad = nt(dy, w_one[wide_rows(at), wide : wide + width]).astype(BF16)
        g_send[:, :, at : at + TILE] = back_grad.reshape(groups, patches, TILE)
        pull.start(at // TILE)
    attended = att_ref[...]
    for at in range(0, width, TILE):
        out = y_first[:, at : at + TILE] + nn(attended, w_two[:, wide + at : wide + at + TILE])
        mixed_ref[:, :, at : at + TILE] = out.astype(BF16).reshape(groups, patches, TILE)

    for block in range(width // LANES):
        at = block * LANES
        if at % TILE == 0:
            pull.wait(at // TILE)
            datt_ref[:, at : at + TILE] = g_recv[:, :, at : at + TILE].reshape(rows, TILE)
        query, keyed, valued = (part_at(qkv_ref, piece, at) for piece in range(3))
        probs = probs_ref[block * stacked : (block + 1) * stacked, :]
        grad = datt_ref[:, at : at + LANES]
        for piece, pulled in enumerate(space.pull(probs, query, keyed, valued, grad)):
            dqkv_ref[:, piece * width + at : piece * width + at + LANES] = pulled
    for at in range(0, width, TILE):
        grad = nt(dqkv_ref[...], w_one[wide_rows(at), 0:wide]).astype(BF16)
        h_send[:, :, at : at + TILE] = grad.reshape(groups, patches, TILE)
        home.start(at // TILE)
    own = x_send[...].reshape(rows, width).astype(F32)
    inv, _ = rms_parts(own)
    for gather in (one, two):
        gather.drain()
    for tile in range(home.tiles):
        home.wait(tile)
    first = rms_pull(own, inv, h_recv[...].reshape(rows, width).astype(F32)).astype(BF16)
    grad_ref[...] = (dy_ref[...] + first).reshape(groups, patches, width)
    for exchange in (bands, back, pull, home):
        exchange.drain()


def wide_rows(at):
    return slice(at, at + TILE)


def local_bands(tokens, cotangent, w_sqkv, w_so, w_gqkv, w_go, keep):
    patches, groups, width = tokens.shape
    rows = patches * groups
    head = width // H
    count = lax.axis_size("grid")
    depth = w_sqkv.shape[0]
    banded = (groups, patches, width)
    flat, wide = (rows, width), (rows, 3 * width)
    full = (depth * count, 4 * width)
    shapes = [full, full, tokens.shape, tokens.shape]
    shapes += [banded] * 8
    shapes += [banded, flat, wide, wide, flat, flat]
    anywhere = pl.BlockSpec(memory_space=pl.ANY)
    vmem = pl.BlockSpec(memory_space=pltpu.VMEM)
    product = 2 * rows * width * width
    mixed, grad = pl.pallas_call(
        partial(layer_kernel, head),
        in_specs=[anywhere] * 6 + [vmem],
        out_specs=(vmem, vmem),
        out_shape=(jax.ShapeDtypeStruct(banded, BF16),) * 2,
        scratch_shapes=[pltpu.VMEM(shape, BF16) for shape in shapes]
        + [pltpu.VMEM((H * rows, rows), F32)]
        + [pltpu.SemaphoreType.DMA((TRANSFERS + 32,)), pltpu.SemaphoreType.DMA((TRANSFERS,))] * 2
        + [pltpu.SemaphoreType.DMA((4, 2)), pltpu.SemaphoreType.DMA((4, 2)), pltpu.SemaphoreType.DMA((6,))]
        + [pltpu.SemaphoreType.REGULAR((6,))],
        compiler_params=pltpu.CompilerParams(
            collective_id=0, has_side_effects=True, vmem_limit_bytes=60 * 2**20
        ),
        cost_estimate=pl.CostEstimate(
            flops=21 * product, bytes_accessed=2**20, transcendentals=0
        ),
    )(tokens, cotangent, w_sqkv, w_so, w_gqkv, w_go, keep)
    return mixed.transpose(1, 0, 2), grad.transpose(1, 0, 2)


def local(tokens, *rest):
    if lax.axis_size("grid") == tokens.shape[1]:
        return local_bands(tokens, *rest)
    return local_any(tokens, *rest)


def solution(mesh):
    placed = (
        P(("parts", "grid"), None, None),
        P(("parts", "grid"), None, None),
        P("grid", None),
        P("grid", None),
        P("grid", None),
        P("grid", None),
        P(None, "parts"),
    )
    return jax.shard_map(
        local,
        mesh=mesh,
        in_specs=placed,
        out_specs=(P(("parts", "grid"), None, None), P(("parts", "grid"), None, None)),
        check_vma=False,
    )
```

```python
from functools import partial

import jax
import jax.numpy as jnp
from jax import lax
from jax.experimental import pallas as pl
from jax.experimental.pallas import tpu as pltpu
from jax.sharding import PartitionSpec as P

H = 16
G = 32


def rms_normalize(values):
    wide = values.astype(jnp.float32)
    meansq = jnp.mean(wide * wide, axis=-1, keepdims=True)
    return (wide * lax.rsqrt(meansq + 1e-06)).astype(jnp.bfloat16)


def project_spatial(tokens, weight):
    patches, groups, width = tokens.shape
    normed = rms_normalize(tokens).reshape(patches * groups, width)
    stacked = jnp.dot(normed, weight, preferred_element_type=jnp.float32).astype(jnp.bfloat16)
    stacked = stacked.reshape(patches, groups, 3, width).transpose(2, 0, 1, 3)
    return stacked.reshape(3, patches, groups * width)


def pair_attention(operands):
    stacked, keep_row = operands
    query, keyed, valued = (stacked[0], stacked[1], stacked[2])
    scale = query.shape[-1] ** (-0.5)
    scores = jnp.dot(query, keyed.T, preferred_element_type=jnp.float32) * scale
    weights = jnp.exp(scores) * keep_row[None, :]
    probs = (weights / jnp.sum(weights, axis=-1, keepdims=True)).astype(jnp.bfloat16)
    return jnp.dot(probs, valued, preferred_element_type=jnp.float32).astype(jnp.bfloat16)


def spatial_attention(stacked, keep_rows, attend):
    three, patches, columns = stacked.shape
    pairs = keep_rows.shape[0]
    split = stacked.reshape(3, patches, pairs, columns // pairs).transpose(2, 0, 1, 3)
    result = lax.map(attend, (split, keep_rows))
    return result.transpose(1, 0, 2).reshape(patches, columns)


def block_group(tokens, attended, w_so, w_gqkv, w_go):
    patches, groups, width = tokens.shape
    rows = patches * groups
    heads = H
    y_first = (
        tokens.reshape(rows, width).astype(jnp.float32)
        + jnp.dot(attended.reshape(rows, width), w_so, preferred_element_type=jnp.float32)
    ).astype(jnp.bfloat16)
    normed = rms_normalize(y_first)
    stacked = jnp.dot(normed, w_gqkv, preferred_element_type=jnp.float32).astype(jnp.bfloat16)
    stacked = stacked.reshape(patches, groups, 3, heads, width // heads)
    query = stacked[:, :, 0].astype(jnp.float32)
    keyed = stacked[:, :, 1].astype(jnp.float32)
    valued = stacked[:, :, 2].astype(jnp.float32)
    scale = (width // heads) ** (-0.5)
    scores = jnp.einsum("pgne,pkne->pngk", query, keyed) * scale
    weights = jnp.exp(scores)
    probs = (weights / jnp.sum(weights, axis=-1, keepdims=True)).astype(jnp.bfloat16)
    result = jnp.einsum("pngk,pkne->pgne", probs.astype(jnp.float32), valued).astype(jnp.bfloat16)
    result = result.reshape(rows, width)
    mixed = (
        y_first.astype(jnp.float32) + jnp.dot(result, w_go, preferred_element_type=jnp.float32)
    ).astype(jnp.bfloat16)
    return mixed.reshape(patches, groups, width)


def local_any(tokens, cotangent, w_sqkv, w_so, w_gqkv, w_go, keep):
    grid_size = lax.axis_size("grid")
    position = lax.axis_index("grid")
    full_sqkv, full_so, full_gqkv, full_go = (
        lax.all_gather(w_sqkv, "grid", axis=0, tiled=True),
        lax.all_gather(w_so, "grid", axis=0, tiled=True),
        lax.all_gather(w_gqkv, "grid", axis=0, tiled=True),
        lax.all_gather(w_go, "grid", axis=0, tiled=True),
    )
    stacked, pull_first = jax.vjp(partial(project_spatial, weight=full_sqkv), tokens)
    banded = lax.all_to_all(stacked, "grid", split_axis=2, concat_axis=1, tiled=True)
    pairs = G * H // grid_size
    pair_ids = position * pairs + jnp.arange(pairs, dtype=jnp.int32)
    select = (pair_ids[:, None] // H == jnp.arange(G, dtype=jnp.int32)[None, :]).astype(jnp.float32)
    keep_rows = jnp.dot(select, keep.astype(jnp.float32), precision=lax.Precision.HIGHEST)
    attend = jax.checkpoint(pair_attention)
    attended_bands, pull_spatial = jax.vjp(
        partial(spatial_attention, keep_rows=keep_rows, attend=attend), banded
    )
    attended = lax.all_to_all(attended_bands, "grid", split_axis=0, concat_axis=1, tiled=True)
    mixed, pull_group = jax.vjp(
        partial(block_group, w_so=full_so, w_gqkv=full_gqkv, w_go=full_go), tokens, attended
    )
    grad_direct, grad_attended = pull_group(cotangent)
    grad_bands = lax.all_to_all(grad_attended, "grid", split_axis=1, concat_axis=0, tiled=True)
    (grad_banded,) = pull_spatial(grad_bands)
    grad_stacked = lax.all_to_all(grad_banded, "grid", split_axis=1, concat_axis=2, tiled=True)
    (grad_first,) = pull_first(grad_stacked)
    return (mixed, grad_direct + grad_first)

F32 = jnp.float32
BF16 = jnp.bfloat16
LANES = 128
EPS = 1e-06
TILE = 512
SPLIT = (2, 2, 2)
TRANSFERS = 93
LAG = 12
PUMP_FROM = 12
PUMP_EVERY = 1
PUMP_BLOCK = 0
PUMP_TURN = 1
MESH = pl.DeviceIdType.MESH


def nn(a, b):
    return lax.dot_general(a, b, (((1,), (0,)), ((), ())), preferred_element_type=F32)


def nt(a, b):
    return lax.dot_general(a, b, (((1,), (1,)), ((), ())), preferred_element_type=F32)


def tn(a, b):
    return lax.dot_general(a, b, (((0,), (0,)), ((), ())), preferred_element_type=F32)


def rms_parts(wide):
    inv = lax.rsqrt(jnp.mean(wide * wide, axis=-1, keepdims=True) + EPS)
    return inv, (wide * inv).astype(BF16)


def rms_pull(wide, inv, grad):
    inner = jnp.mean(grad * wide, axis=-1, keepdims=True)
    return grad * inv - wide * (inv * inv * inv * inner)


class Heads:
    def __init__(self, head, rows, mask):
        lane = lax.broadcasted_iota(jnp.int32, (1, LANES), 1)
        self.count = LANES // head
        self.rows = rows
        scale = head ** (-0.5)
        plain = [(lane // head == index).astype(F32) for index in range(self.count)]
        self.plain = [one.astype(BF16) for one in plain]
        self.scaled = [(one * scale).astype(BF16) for one in plain]
        self.mask = jnp.concatenate([mask] * self.count, axis=0)

    def stack(self, block, selects):
        return jnp.concatenate([block * select for select in selects], axis=0)

    def beside(self, stacked):
        rows = self.rows
        return jnp.concatenate(
            [stacked[at * rows : (at + 1) * rows] for at in range(self.count)], axis=1
        )

    def probs(self, query, keyed):
        scores = nt(self.stack(query, self.scaled), keyed)
        weights = jnp.where(self.mask, jnp.exp(scores), 0.0)
        return weights * (1.0 / jnp.sum(weights, axis=-1, keepdims=True))

    def attend(self, probs, valued):
        return nn(self.beside(probs.astype(BF16)), self.stack(valued, self.plain)).astype(BF16)

    def pull(self, probs, query, keyed, valued, grad):
        grads = self.stack(grad, self.plain)
        dprobs = nt(grads, valued).astype(BF16).astype(F32)
        inner = jnp.sum(dprobs * probs, axis=-1, keepdims=True)
        dscores = (probs * (dprobs - inner)).astype(BF16)
        dquery = nn(self.beside(dscores), self.stack(keyed, self.scaled))
        dkeyed = tn(dscores, self.stack(query, self.scaled))
        dvalued = tn(probs.astype(BF16), grads)
        return dquery.astype(BF16), dkeyed.astype(BF16), dvalued.astype(BF16)


def part_cuts(columns):
    unit = columns // 32
    return ((0, 13 * unit), (13 * unit, 26 * unit), (26 * unit, columns))


class Gather:
    def __init__(self, full_ref, rows, send_sems, recv_sems):
        self.full, self.rows = full_ref, rows
        self.send_sems, self.recv_sems = send_sems, recv_sems
        self.cuts = part_cuts(full_ref.shape[1])
        self.part, self.me = lax.axis_index("parts"), lax.axis_index("grid")
        me = self.me
        self.core, self.x, self.y, self.z = me % 2, (me // 2) % 2, (me // 4) % 2, me // 8
        z = self.z
        self.origins = (z, z + 1 - 2 * (z % 2), 2 - z // 2, 3 * (1 - z // 2))
        self.inner = (z + 1) // 2 == 1
        self.outward = self.place(z + 1 - 2 * (z % 2))
        self.inward = self.place(3 - z)
        self.xp, self.yp = self.place(z, x=1), self.place(z, y=1)
        self.cp = self.place(z, core=1)
        self.sends, self.recvs = {}, {}
        self.sent, self.sent_inner = [], []

    def place(self, z, y=0, x=0, core=0):
        ny, nx, nc = SPLIT
        y = 1 - self.y if y else self.y
        x = 1 - self.x if x else self.x
        core = 1 - self.core if core else self.core
        return ((z * ny + y) * nx + x) * nc + core

    def region(self, piece, owner):
        low, high = self.cuts[piece]
        rows = self.rows
        return self.full.at[pl.ds(pl.multiple_of(owner * rows, rows), rows), low:high]

    def copy(self, name, way, piece, owner, peer):
        at = self.sends.setdefault((name, way), len(self.sends))
        got = self.recvs.setdefault(name, len(self.recvs))
        return pltpu.make_async_remote_copy(
            src_ref=self.region(piece, owner),
            dst_ref=self.region(piece, owner),
            send_sem=self.send_sems.at[at],
            recv_sem=self.recv_sems.at[got],
            device_id=(self.part, peer),
            device_id_type=MESH,
        )

    def send(self, name, piece, owner, peer):
        made = self.copy(name, 0, piece, owner, peer)
        made.start()
        self.sent.append(made)

    def send_inner(self, name, way, piece, owner, peer):
        made = self.copy(name, way, piece, owner, peer)
        pl.when(self.inner)(made.start)
        self.sent_inner.append(made)

    def arrive(self, name, piece, owner):
        got = self.recvs.setdefault(name, len(self.recvs))
        region = self.region(piece, owner)
        pltpu.make_async_remote_copy(
            src_ref=region,
            dst_ref=region,
            send_sem=self.send_sems.at[0],
            recv_sem=self.recv_sems.at[got],
            device_id=(self.part, self.xp),
            device_id_type=MESH,
        ).wait_recv()

    def owner(self, half, j, first, second):
        cross_y, cross_x = (first, second) if half == 0 else (second, first)
        return self.place(self.origins[j], y=cross_y, x=cross_x)

    def peers(self, half):
        return (self.yp, self.xp) if half == 0 else (self.xp, self.yp)

    def z_own(self, tag, piece, owner):
        self.send((tag, 1), piece, owner, self.outward)
        self.send_inner((tag, 2), 1, piece, owner, self.inward)

    def z_pass(self, tag, piece, owner, j):
        if j == 1:
            self.send_inner((tag, 3), 1, piece, owner, self.inward)
        else:
            self.send_inner((tag, j), 2, piece, owner, self.outward)

    def spread_line(self, half, j):
        mine = self.owner(half, j, 0, 0)
        if j:
            self.arrive((("z", half), j), half, mine)
            self.z_pass(("z", half), half, mine, j)
        self.send(("first", half, j), half, mine, self.peers(half)[0])
        self.send(("second", half, j, 0), half, mine, self.peers(half)[1])
        self.send(("core", half, j, 0, 0), half, mine, self.cp)

    def spread_first(self, half, j):
        got = self.owner(half, j, 1, 0)
        self.arrive(("first", half, j), half, got)
        self.send(("second", half, j, 1), half, got, self.peers(half)[1])
        self.send(("core", half, j, 1, 0), half, got, self.cp)

    def spread_second(self, half, j, first):
        got = self.owner(half, j, first, 1)
        self.arrive(("second", half, j, first), half, got)
        self.send(("core", half, j, first, 1), half, got, self.cp)

    def flat_owner(self, j, y, x):
        return self.place(self.origins[j], y=y, x=x)

    def flat_x(self):
        got = self.flat_owner(0, 0, 1)
        self.arrive(("flat x",), 2, got)
        self.send(("flat y", 1), 2, got, self.yp)
        self.z_own(("flat z", 0, 1), 2, got)
        self.send(("flat core", 0, 0, 1), 2, got, self.cp)

    def flat_y(self, x):
        got = self.flat_owner(0, 1, x)
        self.arrive(("flat y", x), 2, got)
        self.z_own(("flat z", 1, x), 2, got)
        self.send(("flat core", 0, 1, x), 2, got, self.cp)

    def flat_z(self, j, y, x):
        got = self.flat_owner(j, y, x)
        tag = ("flat z", y, x)
        self.arrive((tag, j), 2, got)
        self.z_pass(tag, 2, got, j)
        self.send(("flat core", j, y, x), 2, got, self.cp)

    def start(self):
        me = self.me
        for half in range(2):
            self.z_own(("z", half), half, me)
        self.send(("flat x",), 2, me, self.xp)
        for half in range(2):
            self.spread_line(half, 0)
        self.send(("flat y", 0), 2, me, self.yp)
        self.z_own(("flat z", 0, 0), 2, me)
        self.send(("flat core", 0, 0, 0), 2, me, self.cp)

    def steps(self):
        halves = range(2)
        plane = [(0, 0), (0, 1), (1, 0), (1, 1)]
        work = [partial(self.flat_x)]
        work += [partial(self.spread_first, half, 0) for half in halves]
        work += [partial(self.flat_y, x) for x in range(2)]
        for j in range(1, 4):
            work += [partial(self.spread_line, half, j) for half in halves]
            work += [partial(self.spread_second, half, j - 1, 0) for half in halves]
            work += [partial(self.spread_second, half, j - 1, 1) for half in halves]
            work += [partial(self.spread_first, half, j) for half in halves]
            work += [partial(self.flat_z, j, y, x) for y, x in plane]
        work += [partial(self.spread_second, half, 3, 0) for half in halves]
        work += [partial(self.spread_second, half, 3, 1) for half in halves]
        return work

    def finish(self):
        for j in range(4):
            for first in range(2):
                for second in range(2):
                    for half in range(2):
                        cross_y, cross_x = (first, second) if half == 0 else (second, first)
                        got = self.place(self.origins[j], y=cross_y, x=cross_x, core=1)
                        self.arrive(("core", half, j, first, second), half, got)
                    got = self.place(self.origins[j], y=first, x=second, core=1)
                    self.arrive(("flat core", j, first, second), 2, got)

    def drain(self):
        for made in self.sent:
            made.wait_send()

        @pl.when(self.inner)
        def _():
            for made in self.sent_inner:
                made.wait_send()


class Exchange:
    def __init__(self, src, dst, send_sems, recv_sems, tiles=1):
        self.src, self.dst, self.send_sems, self.recv_sems = src, dst, send_sems, recv_sems
        self.part, self.me = lax.axis_index("parts"), lax.axis_index("grid")
        self.count, self.tiles = src.shape[0], tiles
        self.wide = src.shape[2] // tiles

    def columns(self, tile):
        return slice(tile * self.wide, (tile + 1) * self.wide)

    def start(self, tile=0):
        me, count, columns = self.me, self.count, self.columns(tile)

        def one(step, carry):
            peer = (me + step) % count
            pltpu.make_async_remote_copy(
                src_ref=self.src.at[peer, :, columns],
                dst_ref=self.dst.at[me, :, columns],
                send_sem=self.send_sems.at[tile],
                recv_sem=self.recv_sems.at[tile],
                device_id=(self.part, peer),
                device_id_type=MESH,
            ).start()
            return carry

        lax.fori_loop(1, count, one, 0)
        self.dst[pl.ds(me, 1), :, columns] = self.src[pl.ds(me, 1), :, columns]

    def whole(self, tile):
        most, columns = self.count - 1, self.columns(tile)
        return pltpu.make_async_remote_copy(
            src_ref=self.src.at[0:most, :, columns],
            dst_ref=self.dst.at[0:most, :, columns],
            send_sem=self.send_sems.at[tile],
            recv_sem=self.recv_sems.at[tile],
            device_id=(self.part, (self.me + 1) % self.count),
            device_id_type=MESH,
        )

    def wait(self, tile=0):
        self.whole(tile).wait_recv()

    def drain(self):
        for tile in range(self.tiles):
            self.whole(tile).wait_send()


class Greeting:
    def __init__(self, gather, sems):
        self.at, self.sems = gather, sems

    def signal(self, sem, peer):
        pl.semaphore_signal(
            sem, inc=1, device_id=(self.at.part, peer), device_id_type=MESH
        )

    def neighbours(self):
        at, barrier = self.at, pltpu.get_barrier_semaphore()
        for peer in (at.xp, at.yp, at.cp, at.outward):
            self.signal(barrier, peer)

        @pl.when(at.inner)
        def _():
            self.signal(barrier, at.inward)

    def meet(self):
        at, barrier = self.at, pltpu.get_barrier_semaphore()
        pl.semaphore_wait(barrier, 4 + jnp.where(at.inner, 1, 0))
        self.signal(self.sems.at[0], at.cp)

    def stages(self):
        at, sems = self.at, self.sems
        order = (at.cp, at.xp, at.yp, at.outward)

        def pass_on(stage):
            pl.semaphore_wait(sems.at[stage], 1)
            self.signal(sems.at[stage + 1], order[stage + 1])

        def across():
            pl.semaphore_wait(sems.at[3], 1)

            @pl.when(at.inner)
            def _():
                self.signal(sems.at[4], at.inward)

        def ends():
            @pl.when(at.inner)
            def _():
                pl.semaphore_wait(sems.at[4], 1)
                self.signal(sems.at[5], at.outward)

            @pl.when(jnp.logical_not(at.inner))
            def _():
                pl.semaphore_wait(sems.at[5], 1)

        return [partial(pass_on, stage) for stage in range(3)] + [across, ends]


def layer_kernel(
    head,
    tok_hbm, cot_hbm, sqkv_hbm, so_hbm, gqkv_hbm, go_hbm, keep_ref,
    mixed_ref, grad_ref,
    w_one, w_two, tok_ref, cot_ref,
    x_send, x_recv, y_send, y_recv, g_send, g_recv, h_send, h_recv,
    cot_mine, dy_ref, qkv_ref, dqkv_ref, att_ref, datt_ref, w_back, probs_ref, sum_ref,
    send_one, recv_one, send_two, recv_two, a2a_send, a2a_recv, own_sems, hello,
):
    count = lax.axis_size("grid")
    part, me = lax.axis_index("parts"), lax.axis_index("grid")
    patches, groups, width = tok_ref.shape
    rows = patches * groups
    wide = 3 * width
    depth = sqkv_hbm.shape[0]
    mine = pl.ds(pl.multiple_of(me * depth, depth), depth)
    loads = [
        pltpu.make_async_copy(source, target, own_sems.at[at])
        for at, (source, target) in enumerate((
            (sqkv_hbm, w_one.at[mine, 0:wide]),
            (so_hbm, w_one.at[mine, wide : wide + width]),
            (gqkv_hbm, w_two.at[mine, 0:wide]),
            (go_hbm, w_two.at[mine, wide : wide + width]),
            (tok_hbm, tok_ref),
            (cot_hbm, cot_ref),
        ))
    ]
    for load in loads:
        load.start()

    one = Gather(w_one, depth, send_one, recv_one)
    two = Gather(w_two, depth, send_two, recv_two)
    greeting = Greeting(one, hello)
    bands = Exchange(x_send, x_recv, a2a_send.at[0], a2a_recv.at[0])
    back = Exchange(y_send, y_recv, a2a_send.at[1], a2a_recv.at[1])
    pull = Exchange(g_send, g_recv, a2a_send.at[2], a2a_recv.at[2], width // TILE)
    home = Exchange(h_send, h_recv, a2a_send.at[3], a2a_recv.at[3], width // TILE)

    greeting.neighbours()
    for load in loads[:4]:
        load.wait()
    greeting.meet()
    one.start()
    loads[4].wait()
    for at in range(patches):
        x_send[:, at, :] = tok_ref[at]
    loads[5].wait()
    for at in range(patches):
        cot_mine[:, at, :] = cot_ref[at]
    stages = greeting.stages()
    ahead = two.steps()

    def pump(steps):
        for _ in range(min(steps, len(ahead))):
            ahead.pop(0)()

    for at, step in enumerate(one.steps()):
        if at < len(stages):
            stages[at]()
        step()
        if at == len(stages):
            bands.start()
        if at == LAG:
            two.start()
        if at > PUMP_FROM and at % PUMP_EVERY == 0:
            pump(1)
    one.finish()
    bands.wait()

    def part_at(ref, piece, at):
        return ref[:, piece * width + at : piece * width + at + LANES]

    x = x_recv[...].reshape(rows, width).astype(F32)
    _, normed = rms_parts(x)
    for at in range(0, wide, TILE):
        qkv_ref[:, at : at + TILE] = nn(normed, w_one[:, at : at + TILE]).astype(BF16)
    pump(PUMP_BLOCK)
    keep_row = keep_ref[pl.ds(me, 1), :]
    space = Heads(head, rows, jnp.broadcast_to(keep_row, (rows, rows)) > 0)
    stacked = space.count * rows
    for block in range(width // LANES):
        at = block * LANES
        query, keyed, valued = (part_at(qkv_ref, piece, at) for piece in range(3))
        probs = space.probs(query, keyed)
        probs_ref[block * stacked : (block + 1) * stacked, :] = probs
        att_ref[:, at : at + LANES] = space.attend(probs, valued)
        pump(PUMP_BLOCK)
    attended = att_ref[...]
    for at in range(0, width, TILE):
        y = x[:, at : at + TILE] + nn(attended, w_one[:, wide + at : wide + at + TILE])
        y_send[:, :, at : at + TILE] = y.astype(BF16).reshape(groups, patches, TILE)
    back.start()
    for at in range(0, wide + width, LANES):
        w_back[at : at + LANES, :] = w_one[:, at : at + LANES].T
        if at % TILE == 0:
            pump(PUMP_TURN)
    pump(len(ahead))
    two.finish()

    cot = cot_mine[...].reshape(rows, width)
    for at in range(0, width, TILE):
        datt_ref[:, at : at + TILE] = nt(cot, w_two[wide_rows(at), wide : wide + width]).astype(BF16)
    back.wait()
    y_first = y_recv[...].reshape(rows, width).astype(F32)
    inv, normed = rms_parts(y_first)
    for at in range(0, wide, TILE):
        dqkv_ref[:, at : at + TILE] = nn(normed, w_two[:, at : at + TILE]).astype(BF16)
    row = lax.broadcasted_iota(jnp.int32, (rows, rows), 0)
    col = lax.broadcasted_iota(jnp.int32, (rows, rows), 1)
    across = Heads(head, rows, row % patches == col % patches)
    for block in range(width // LANES):
        at = block * LANES
        query, keyed, valued = (part_at(dqkv_ref, piece, at) for piece in range(3))
        grad = datt_ref[:, at : at + LANES]
        probs = across.probs(query, keyed)
        att_ref[:, at : at + LANES] = across.attend(probs, valued)
        for piece, pulled in enumerate(across.pull(probs, query, keyed, valued, grad)):
            dqkv_ref[:, piece * width + at : piece * width + at + LANES] = pulled
    for at in range(0, width, TILE):
        datt_ref[:, at : at + TILE] = nt(dqkv_ref[...], w_two[wide_rows(at), 0:wide]).astype(BF16)
    dy = cot + rms_pull(y_first, inv, datt_ref[...].astype(F32)).astype(BF16)
    dy_ref[...] = dy
    for at in range(0, width, TILE):
        back_grad = nn(dy, w_back[wide : wide + width, wide_rows(at)]).astype(BF16)
        g_send[:, :, at : at + TILE] = back_grad.reshape(groups, patches, TILE)
        pull.start(at // TILE)
    attended = att_ref[...]
    for at in range(0, width, TILE):
        out = y_first[:, at : at + TILE] + nn(attended, w_two[:, wide + at : wide + at + TILE])
        mixed_ref[:, :, at : at + TILE] = out.astype(BF16).reshape(groups, patches, TILE)

    def through(low, high, at):
        total = 0.0
        for piece in range(3):
            here = slice(piece * width + low, piece * width + high)
            total = total + nn(dqkv_ref[:, here], w_back[here, at : at + TILE])
        return total

    for block in range(width // LANES):
        at = block * LANES
        if at % TILE == 0:
            if at == TILE:
                for column in range(0, width, TILE):
                    sum_ref[:, column : column + TILE] = through(0, TILE, column)
            pull.wait(at // TILE)
            datt_ref[:, at : at + TILE] = g_recv[:, :, at : at + TILE].reshape(rows, TILE)
        query, keyed, valued = (part_at(qkv_ref, piece, at) for piece in range(3))
        probs = probs_ref[block * stacked : (block + 1) * stacked, :]
        grad = datt_ref[:, at : at + LANES]
        for piece, pulled in enumerate(space.pull(probs, query, keyed, valued, grad)):
            dqkv_ref[:, piece * width + at : piece * width + at + LANES] = pulled
    for at in range(0, width, TILE):
        grad = (sum_ref[:, at : at + TILE] + through(TILE, width, at)).astype(BF16)
        h_send[:, :, at : at + TILE] = grad.reshape(groups, patches, TILE)
        home.start(at // TILE)
    own = x_send[...].reshape(rows, width).astype(F32)
    inv, _ = rms_parts(own)
    for gather in (one, two):
        gather.drain()
    for tile in range(home.tiles):
        home.wait(tile)
    first = rms_pull(own, inv, h_recv[...].reshape(rows, width).astype(F32)).astype(BF16)
    grad_ref[...] = (dy_ref[...] + first).reshape(groups, patches, width)
    for exchange in (bands, back, pull, home):
        exchange.drain()


def wide_rows(at):
    return slice(at, at + TILE)


def local_bands(tokens, cotangent, w_sqkv, w_so, w_gqkv, w_go, keep):
    patches, groups, width = tokens.shape
    rows = patches * groups
    head = width // H
    count = lax.axis_size("grid")
    depth = w_sqkv.shape[0]
    banded = (groups, patches, width)
    flat, wide = (rows, width), (rows, 3 * width)
    full = (depth * count, 4 * width)
    shapes = [full, full, tokens.shape, tokens.shape]
    shapes += [banded] * 8
    shapes += [banded, flat, wide, wide, flat, flat, (4 * width, full[0])]
    anywhere = pl.BlockSpec(memory_space=pl.ANY)
    vmem = pl.BlockSpec(memory_space=pltpu.VMEM)
    product = 2 * rows * width * width
    mixed, grad = pl.pallas_call(
        partial(layer_kernel, head),
        in_specs=[anywhere] * 6 + [vmem],
        out_specs=(vmem, vmem),
        out_shape=(jax.ShapeDtypeStruct(banded, BF16),) * 2,
        scratch_shapes=[pltpu.VMEM(shape, BF16) for shape in shapes]
        + [pltpu.VMEM((H * rows, rows), F32), pltpu.VMEM(flat, F32)]
        + [pltpu.SemaphoreType.DMA((TRANSFERS + 32,)), pltpu.SemaphoreType.DMA((TRANSFERS,))] * 2
        + [pltpu.SemaphoreType.DMA((4, 2)), pltpu.SemaphoreType.DMA((4, 2)), pltpu.SemaphoreType.DMA((6,))]
        + [pltpu.SemaphoreType.REGULAR((6,))],
        compiler_params=pltpu.CompilerParams(
            collective_id=0, has_side_effects=True, vmem_limit_bytes=60 * 2**20
        ),
        cost_estimate=pl.CostEstimate(
            flops=21 * product, bytes_accessed=2**20, transcendentals=0
        ),
    )(tokens, cotangent, w_sqkv, w_so, w_gqkv, w_go, keep)
    return mixed.transpose(1, 0, 2), grad.transpose(1, 0, 2)


def local(tokens, *rest):
    if lax.axis_size("grid") == tokens.shape[1]:
        return local_bands(tokens, *rest)
    return local_any(tokens, *rest)


def solution(mesh):
    placed = (
        P(("parts", "grid"), None, None),
        P(("parts", "grid"), None, None),
        P("grid", None),
        P("grid", None),
        P("grid", None),
        P("grid", None),
        P(None, "parts"),
    )
    return jax.shard_map(
        local,
        mesh=mesh,
        in_specs=placed,
        out_specs=(P(("parts", "grid"), None, None), P(("parts", "grid"), None, None)),
        check_vma=False,
    )
```

```python
from functools import partial

import jax
import jax.numpy as jnp
from jax import lax
from jax.experimental import pallas as pl
from jax.experimental.pallas import tpu as pltpu
from jax.sharding import PartitionSpec as P

H = 16
G = 32


def rms_normalize(values):
    wide = values.astype(jnp.float32)
    meansq = jnp.mean(wide * wide, axis=-1, keepdims=True)
    return (wide * lax.rsqrt(meansq + 1e-06)).astype(jnp.bfloat16)


def project_spatial(tokens, weight):
    patches, groups, width = tokens.shape
    normed = rms_normalize(tokens).reshape(patches * groups, width)
    stacked = jnp.dot(normed, weight, preferred_element_type=jnp.float32).astype(jnp.bfloat16)
    stacked = stacked.reshape(patches, groups, 3, width).transpose(2, 0, 1, 3)
    return stacked.reshape(3, patches, groups * width)


def pair_attention(operands):
    stacked, keep_row = operands
    query, keyed, valued = (stacked[0], stacked[1], stacked[2])
    scale = query.shape[-1] ** (-0.5)
    scores = jnp.dot(query, keyed.T, preferred_element_type=jnp.float32) * scale
    weights = jnp.exp(scores) * keep_row[None, :]
    probs = (weights / jnp.sum(weights, axis=-1, keepdims=True)).astype(jnp.bfloat16)
    return jnp.dot(probs, valued, preferred_element_type=jnp.float32).astype(jnp.bfloat16)


def spatial_attention(stacked, keep_rows, attend):
    three, patches, columns = stacked.shape
    pairs = keep_rows.shape[0]
    split = stacked.reshape(3, patches, pairs, columns // pairs).transpose(2, 0, 1, 3)
    result = lax.map(attend, (split, keep_rows))
    return result.transpose(1, 0, 2).reshape(patches, columns)


def block_group(tokens, attended, w_so, w_gqkv, w_go):
    patches, groups, width = tokens.shape
    rows = patches * groups
    heads = H
    y_first = (
        tokens.reshape(rows, width).astype(jnp.float32)
        + jnp.dot(attended.reshape(rows, width), w_so, preferred_element_type=jnp.float32)
    ).astype(jnp.bfloat16)
    normed = rms_normalize(y_first)
    stacked = jnp.dot(normed, w_gqkv, preferred_element_type=jnp.float32).astype(jnp.bfloat16)
    stacked = stacked.reshape(patches, groups, 3, heads, width // heads)
    query = stacked[:, :, 0].astype(jnp.float32)
    keyed = stacked[:, :, 1].astype(jnp.float32)
    valued = stacked[:, :, 2].astype(jnp.float32)
    scale = (width // heads) ** (-0.5)
    scores = jnp.einsum("pgne,pkne->pngk", query, keyed) * scale
    weights = jnp.exp(scores)
    probs = (weights / jnp.sum(weights, axis=-1, keepdims=True)).astype(jnp.bfloat16)
    result = jnp.einsum("pngk,pkne->pgne", probs.astype(jnp.float32), valued).astype(jnp.bfloat16)
    result = result.reshape(rows, width)
    mixed = (
        y_first.astype(jnp.float32) + jnp.dot(result, w_go, preferred_element_type=jnp.float32)
    ).astype(jnp.bfloat16)
    return mixed.reshape(patches, groups, width)


def local_any(tokens, cotangent, w_sqkv, w_so, w_gqkv, w_go, keep):
    grid_size = lax.axis_size("grid")
    position = lax.axis_index("grid")
    full_sqkv, full_so, full_gqkv, full_go = (
        lax.all_gather(w_sqkv, "grid", axis=0, tiled=True),
        lax.all_gather(w_so, "grid", axis=0, tiled=True),
        lax.all_gather(w_gqkv, "grid", axis=0, tiled=True),
        lax.all_gather(w_go, "grid", axis=0, tiled=True),
    )
    stacked, pull_first = jax.vjp(partial(project_spatial, weight=full_sqkv), tokens)
    banded = lax.all_to_all(stacked, "grid", split_axis=2, concat_axis=1, tiled=True)
    pairs = G * H // grid_size
    pair_ids = position * pairs + jnp.arange(pairs, dtype=jnp.int32)
    select = (pair_ids[:, None] // H == jnp.arange(G, dtype=jnp.int32)[None, :]).astype(jnp.float32)
    keep_rows = jnp.dot(select, keep.astype(jnp.float32), precision=lax.Precision.HIGHEST)
    attend = jax.checkpoint(pair_attention)
    attended_bands, pull_spatial = jax.vjp(
        partial(spatial_attention, keep_rows=keep_rows, attend=attend), banded
    )
    attended = lax.all_to_all(attended_bands, "grid", split_axis=0, concat_axis=1, tiled=True)
    mixed, pull_group = jax.vjp(
        partial(block_group, w_so=full_so, w_gqkv=full_gqkv, w_go=full_go), tokens, attended
    )
    grad_direct, grad_attended = pull_group(cotangent)
    grad_bands = lax.all_to_all(grad_attended, "grid", split_axis=1, concat_axis=0, tiled=True)
    (grad_banded,) = pull_spatial(grad_bands)
    grad_stacked = lax.all_to_all(grad_banded, "grid", split_axis=1, concat_axis=2, tiled=True)
    (grad_first,) = pull_first(grad_stacked)
    return (mixed, grad_direct + grad_first)

F32 = jnp.float32
BF16 = jnp.bfloat16
LANES = 128
EPS = 1e-06
TILE = 512
SPLIT = (2, 2, 2)
TRANSFERS = 93
LAG = 12
PUMP_FROM = 12
PUMP_EVERY = 1
PUMP_BLOCK = 0
PUMP_TURN = 1
MESH = pl.DeviceIdType.MESH


def nn(a, b):
    return lax.dot_general(a, b, (((1,), (0,)), ((), ())), preferred_element_type=F32)


def nt(a, b):
    return lax.dot_general(a, b, (((1,), (1,)), ((), ())), preferred_element_type=F32)


def tn(a, b):
    return lax.dot_general(a, b, (((0,), (0,)), ((), ())), preferred_element_type=F32)


def rms_parts(wide):
    inv = lax.rsqrt(jnp.mean(wide * wide, axis=-1, keepdims=True) + EPS)
    return inv, (wide * inv).astype(BF16)


def rms_pull(wide, inv, grad):
    inner = jnp.mean(grad * wide, axis=-1, keepdims=True)
    return grad * inv - wide * (inv * inv * inv * inner)


class Heads:
    def __init__(self, head, rows, mask):
        lane = lax.broadcasted_iota(jnp.int32, (1, LANES), 1)
        self.count = LANES // head
        self.rows = rows
        scale = head ** (-0.5)
        plain = [(lane // head == index).astype(F32) for index in range(self.count)]
        self.plain = [one.astype(BF16) for one in plain]
        self.scaled = [(one * scale).astype(BF16) for one in plain]
        self.mask = jnp.concatenate([mask] * self.count, axis=0)

    def stack(self, block, selects):
        return jnp.concatenate([block * select for select in selects], axis=0)

    def beside(self, stacked):
        rows = self.rows
        return jnp.concatenate(
            [stacked[at * rows : (at + 1) * rows] for at in range(self.count)], axis=1
        )

    def probs(self, query, keyed):
        scores = nt(self.stack(query, self.scaled), keyed)
        weights = jnp.where(self.mask, jnp.exp(scores), 0.0)
        return weights * (1.0 / jnp.sum(weights, axis=-1, keepdims=True))

    def attend(self, probs, valued):
        return nn(self.beside(probs.astype(BF16)), self.stack(valued, self.plain)).astype(BF16)

    def pull(self, probs, query, keyed, valued, grad):
        grads = self.stack(grad, self.plain)
        dprobs = nt(grads, valued).astype(BF16).astype(F32)
        inner = jnp.sum(dprobs * probs, axis=-1, keepdims=True)
        dscores = (probs * (dprobs - inner)).astype(BF16)
        dquery = nn(self.beside(dscores), self.stack(keyed, self.scaled))
        dkeyed = tn(dscores, self.stack(query, self.scaled))
        dvalued = tn(probs.astype(BF16), grads)
        return dquery.astype(BF16), dkeyed.astype(BF16), dvalued.astype(BF16)


def part_cuts(columns):
    unit = columns // 32
    return ((0, 13 * unit), (13 * unit, 26 * unit), (26 * unit, columns))


class Gather:
    def __init__(self, full_ref, rows, send_sems, recv_sems):
        self.full, self.rows = full_ref, rows
        self.send_sems, self.recv_sems = send_sems, recv_sems
        self.cuts = part_cuts(full_ref.shape[1])
        self.part, self.me = lax.axis_index("parts"), lax.axis_index("grid")
        me = self.me
        self.core, self.x, self.y, self.z = me % 2, (me // 2) % 2, (me // 4) % 2, me // 8
        z = self.z
        self.origins = (z, z + 1 - 2 * (z % 2), 2 - z // 2, 3 * (1 - z // 2))
        self.inner = (z + 1) // 2 == 1
        self.outward = self.place(z + 1 - 2 * (z % 2))
        self.inward = self.place(3 - z)
        self.xp, self.yp = self.place(z, x=1), self.place(z, y=1)
        self.cp = self.place(z, core=1)
        self.sends, self.recvs = {}, {}
        self.sent, self.sent_inner = [], []

    def place(self, z, y=0, x=0, core=0):
        ny, nx, nc = SPLIT
        y = 1 - self.y if y else self.y
        x = 1 - self.x if x else self.x
        core = 1 - self.core if core else self.core
        return ((z * ny + y) * nx + x) * nc + core

    def region(self, piece, owner):
        low, high = self.cuts[piece]
        rows = self.rows
        return self.full.at[pl.ds(pl.multiple_of(owner * rows, rows), rows), low:high]

    def copy(self, name, way, piece, owner, peer):
        at = self.sends.setdefault((name, way), len(self.sends))
        got = self.recvs.setdefault(name, len(self.recvs))
        return pltpu.make_async_remote_copy(
            src_ref=self.region(piece, owner),
            dst_ref=self.region(piece, owner),
            send_sem=self.send_sems.at[at],
            recv_sem=self.recv_sems.at[got],
            device_id=(self.part, peer),
            device_id_type=MESH,
        )

    def send(self, name, piece, owner, peer):
        made = self.copy(name, 0, piece, owner, peer)
        made.start()
        self.sent.append(made)

    def send_inner(self, name, way, piece, owner, peer):
        made = self.copy(name, way, piece, owner, peer)
        pl.when(self.inner)(made.start)
        self.sent_inner.append(made)

    def arrive(self, name, piece, owner):
        got = self.recvs.setdefault(name, len(self.recvs))
        region = self.region(piece, owner)
        pltpu.make_async_remote_copy(
            src_ref=region,
            dst_ref=region,
            send_sem=self.send_sems.at[0],
            recv_sem=self.recv_sems.at[got],
            device_id=(self.part, self.xp),
            device_id_type=MESH,
        ).wait_recv()

    def owner(self, half, j, first, second):
        cross_y, cross_x = (first, second) if half == 0 else (second, first)
        return self.place(self.origins[j], y=cross_y, x=cross_x)

    def peers(self, half):
        return (self.yp, self.xp) if half == 0 else (self.xp, self.yp)

    def z_own(self, tag, piece, owner):
        self.send((tag, 1), piece, owner, self.outward)
        self.send_inner((tag, 2), 1, piece, owner, self.inward)

    def z_pass(self, tag, piece, owner, j):
        if j == 1:
            self.send_inner((tag, 3), 1, piece, owner, self.inward)
        else:
            self.send_inner((tag, j), 2, piece, owner, self.outward)

    def spread_line(self, half, j):
        mine = self.owner(half, j, 0, 0)
        if j:
            self.arrive((("z", half), j), half, mine)
            self.z_pass(("z", half), half, mine, j)
        self.send(("first", half, j), half, mine, self.peers(half)[0])
        self.send(("second", half, j, 0), half, mine, self.peers(half)[1])
        self.send(("core", half, j, 0, 0), half, mine, self.cp)

    def spread_first(self, half, j):
        got = self.owner(half, j, 1, 0)
        self.arrive(("first", half, j), half, got)
        self.send(("second", half, j, 1), half, got, self.peers(half)[1])
        self.send(("core", half, j, 1, 0), half, got, self.cp)

    def spread_second(self, half, j, first):
        got = self.owner(half, j, first, 1)
        self.arrive(("second", half, j, first), half, got)
        self.send(("core", half, j, first, 1), half, got, self.cp)

    def flat_owner(self, j, y, x):
        return self.place(self.origins[j], y=y, x=x)

    def flat_x(self):
        got = self.flat_owner(0, 0, 1)
        self.arrive(("flat x",), 2, got)
        self.send(("flat y", 1), 2, got, self.yp)
        self.z_own(("flat z", 0, 1), 2, got)
        self.send(("flat core", 0, 0, 1), 2, got, self.cp)

    def flat_y(self, x):
        got = self.flat_owner(0, 1, x)
        self.arrive(("flat y", x), 2, got)
        self.z_own(("flat z", 1, x), 2, got)
        self.send(("flat core", 0, 1, x), 2, got, self.cp)

    def flat_z(self, j, y, x):
        got = self.flat_owner(j, y, x)
        tag = ("flat z", y, x)
        self.arrive((tag, j), 2, got)
        self.z_pass(tag, 2, got, j)
        self.send(("flat core", j, y, x), 2, got, self.cp)

    def start(self):
        me = self.me
        for half in range(2):
            self.z_own(("z", half), half, me)
        self.send(("flat x",), 2, me, self.xp)
        for half in range(2):
            self.spread_line(half, 0)
        self.send(("flat y", 0), 2, me, self.yp)
        self.z_own(("flat z", 0, 0), 2, me)
        self.send(("flat core", 0, 0, 0), 2, me, self.cp)

    def steps(self):
        halves = range(2)
        plane = [(0, 0), (0, 1), (1, 0), (1, 1)]
        work = [partial(self.flat_x)]
        work += [partial(self.spread_first, half, 0) for half in halves]
        work += [partial(self.flat_y, x) for x in range(2)]
        for j in range(1, 4):
            work += [partial(self.spread_line, half, j) for half in halves]
            work += [partial(self.spread_second, half, j - 1, 0) for half in halves]
            work += [partial(self.spread_second, half, j - 1, 1) for half in halves]
            work += [partial(self.spread_first, half, j) for half in halves]
            work += [partial(self.flat_z, j, y, x) for y, x in plane]
        work += [partial(self.spread_second, half, 3, 0) for half in halves]
        work += [partial(self.spread_second, half, 3, 1) for half in halves]
        return work

    def finish(self):
        for j in range(4):
            for first in range(2):
                for second in range(2):
                    for half in range(2):
                        cross_y, cross_x = (first, second) if half == 0 else (second, first)
                        got = self.place(self.origins[j], y=cross_y, x=cross_x, core=1)
                        self.arrive(("core", half, j, first, second), half, got)
                    got = self.place(self.origins[j], y=first, x=second, core=1)
                    self.arrive(("flat core", j, first, second), 2, got)

    def drain(self):
        for made in self.sent:
            made.wait_send()

        @pl.when(self.inner)
        def _():
            for made in self.sent_inner:
                made.wait_send()


def flipped(me, bits, count):
    peer, unit = 0, 1
    while unit < count:
        mine, flip = (me // unit) % 2, (bits // unit) % 2
        peer = peer + unit * (mine + flip - 2 * mine * flip)
        unit *= 2
    return peer


class Exchange:
    def __init__(self, src, dst, send_sems, recv_sems, tiles=1):
        self.src, self.dst, self.send_sems, self.recv_sems = src, dst, send_sems, recv_sems
        self.part, self.me = lax.axis_index("parts"), lax.axis_index("grid")
        self.count, self.tiles = src.shape[0], tiles
        self.wide = src.shape[2] // tiles

    def columns(self, tile):
        return slice(tile * self.wide, (tile + 1) * self.wide)

    def start(self, tile=0):
        me, count, columns = self.me, self.count, self.columns(tile)

        def one(step, carry):
            peer = flipped(me, count - step, count)
            pltpu.make_async_remote_copy(
                src_ref=self.src.at[peer, :, columns],
                dst_ref=self.dst.at[me, :, columns],
                send_sem=self.send_sems.at[tile],
                recv_sem=self.recv_sems.at[tile],
                device_id=(self.part, peer),
                device_id_type=MESH,
            ).start()
            return carry

        lax.fori_loop(1, count, one, 0)
        self.dst[pl.ds(me, 1), :, columns] = self.src[pl.ds(me, 1), :, columns]

    def whole(self, tile):
        most, columns = self.count - 1, self.columns(tile)
        return pltpu.make_async_remote_copy(
            src_ref=self.src.at[0:most, :, columns],
            dst_ref=self.dst.at[0:most, :, columns],
            send_sem=self.send_sems.at[tile],
            recv_sem=self.recv_sems.at[tile],
            device_id=(self.part, (self.me + 1) % self.count),
            device_id_type=MESH,
        )

    def wait(self, tile=0):
        self.whole(tile).wait_recv()

    def drain(self):
        for tile in range(self.tiles):
            self.whole(tile).wait_send()


class Greeting:
    def __init__(self, gather, sems):
        self.at, self.sems = gather, sems

    def signal(self, sem, peer):
        pl.semaphore_signal(
            sem, inc=1, device_id=(self.at.part, peer), device_id_type=MESH
        )

    def neighbours(self):
        at, barrier = self.at, pltpu.get_barrier_semaphore()
        for peer in (at.xp, at.yp, at.cp, at.outward):
            self.signal(barrier, peer)

        @pl.when(at.inner)
        def _():
            self.signal(barrier, at.inward)

    def meet(self):
        at, barrier = self.at, pltpu.get_barrier_semaphore()
        pl.semaphore_wait(barrier, 4 + jnp.where(at.inner, 1, 0))
        self.signal(self.sems.at[0], at.cp)

    def stages(self):
        at, sems = self.at, self.sems
        order = (at.cp, at.xp, at.yp, at.outward)

        def pass_on(stage):
            pl.semaphore_wait(sems.at[stage], 1)
            self.signal(sems.at[stage + 1], order[stage + 1])

        def across():
            pl.semaphore_wait(sems.at[3], 1)

            @pl.when(at.inner)
            def _():
                self.signal(sems.at[4], at.inward)

        def ends():
            @pl.when(at.inner)
            def _():
                pl.semaphore_wait(sems.at[4], 1)
                self.signal(sems.at[5], at.outward)

            @pl.when(jnp.logical_not(at.inner))
            def _():
                pl.semaphore_wait(sems.at[5], 1)

        return [partial(pass_on, stage) for stage in range(3)] + [across, ends]


def layer_kernel(
    head,
    tok_hbm, cot_hbm, sqkv_hbm, so_hbm, gqkv_hbm, go_hbm, keep_ref,
    mixed_ref, grad_ref,
    w_one, w_two, tok_ref, cot_ref,
    x_send, x_recv, y_send, y_recv, g_send, g_recv, h_send, h_recv,
    cot_mine, dy_ref, qkv_ref, dqkv_ref, att_ref, datt_ref, w_back, probs_ref, sum_ref,
    send_one, recv_one, send_two, recv_two, a2a_send, a2a_recv, own_sems, hello,
):
    count = lax.axis_size("grid")
    part, me = lax.axis_index("parts"), lax.axis_index("grid")
    patches, groups, width = tok_ref.shape
    rows = patches * groups
    wide = 3 * width
    depth = sqkv_hbm.shape[0]
    mine = pl.ds(pl.multiple_of(me * depth, depth), depth)
    loads = [
        pltpu.make_async_copy(source, target, own_sems.at[at])
        for at, (source, target) in enumerate((
            (sqkv_hbm, w_one.at[mine, 0:wide]),
            (so_hbm, w_one.at[mine, wide : wide + width]),
            (gqkv_hbm, w_two.at[mine, 0:wide]),
            (go_hbm, w_two.at[mine, wide : wide + width]),
            (tok_hbm, tok_ref),
            (cot_hbm, cot_ref),
        ))
    ]
    for load in loads:
        load.start()

    one = Gather(w_one, depth, send_one, recv_one)
    two = Gather(w_two, depth, send_two, recv_two)
    greeting = Greeting(one, hello)
    bands = Exchange(x_send, x_recv, a2a_send.at[0], a2a_recv.at[0])
    back = Exchange(y_send, y_recv, a2a_send.at[1], a2a_recv.at[1])
    pull = Exchange(g_send, g_recv, a2a_send.at[2], a2a_recv.at[2], width // TILE)
    home = Exchange(h_send, h_recv, a2a_send.at[3], a2a_recv.at[3])

    greeting.neighbours()
    for load in loads[:4]:
        load.wait()
    greeting.meet()
    one.start()
    loads[4].wait()
    for at in range(patches):
        x_send[:, at, :] = tok_ref[at]
    loads[5].wait()
    for at in range(patches):
        cot_mine[:, at, :] = cot_ref[at]
    stages = greeting.stages()
    ahead = two.steps()

    def pump(steps):
        for _ in range(min(steps, len(ahead))):
            ahead.pop(0)()

    for at, step in enumerate(one.steps()):
        if at < len(stages):
            stages[at]()
        step()
        if at == len(stages):
            bands.start()
        if at == LAG:
            two.start()
        if at > PUMP_FROM and at % PUMP_EVERY == 0:
            pump(1)
    one.finish()
    bands.wait()

    def part_at(ref, piece, at):
        return ref[:, piece * width + at : piece * width + at + LANES]

    x = x_recv[...].reshape(rows, width).astype(F32)
    _, normed = rms_parts(x)
    for at in range(0, wide, TILE):
        qkv_ref[:, at : at + TILE] = nn(normed, w_one[:, at : at + TILE]).astype(BF16)
    pump(PUMP_BLOCK)
    keep_row = keep_ref[pl.ds(me, 1), :]
    space = Heads(head, rows, jnp.broadcast_to(keep_row, (rows, rows)) > 0)
    stacked = space.count * rows
    for block in range(width // LANES):
        at = block * LANES
        query, keyed, valued = (part_at(qkv_ref, piece, at) for piece in range(3))
        probs = space.probs(query, keyed)
        probs_ref[block * stacked : (block + 1) * stacked, :] = probs
        att_ref[:, at : at + LANES] = space.attend(probs, valued)
        pump(PUMP_BLOCK)
    attended = att_ref[...]
    for at in range(0, width, TILE):
        y = x[:, at : at + TILE] + nn(attended, w_one[:, wide + at : wide + at + TILE])
        y_send[:, :, at : at + TILE] = y.astype(BF16).reshape(groups, patches, TILE)
    back.start()
    for at in range(0, wide + width, LANES):
        w_back[at : at + LANES, :] = w_one[:, at : at + LANES].T
        if at % TILE == 0:
            pump(PUMP_TURN)
    pump(len(ahead))
    two.finish()

    cot = cot_mine[...].reshape(rows, width)
    for at in range(0, width, TILE):
        datt_ref[:, at : at + TILE] = nt(cot, w_two[wide_rows(at), wide : wide + width]).astype(BF16)
    back.wait()
    y_first = y_recv[...].reshape(rows, width).astype(F32)
    inv, normed = rms_parts(y_first)
    for at in range(0, wide, TILE):
        dqkv_ref[:, at : at + TILE] = nn(normed, w_two[:, at : at + TILE]).astype(BF16)
    row = lax.broadcasted_iota(jnp.int32, (rows, rows), 0)
    col = lax.broadcasted_iota(jnp.int32, (rows, rows), 1)
    across = Heads(head, rows, row % patches == col % patches)
    for block in range(width // LANES):
        at = block * LANES
        query, keyed, valued = (part_at(dqkv_ref, piece, at) for piece in range(3))
        grad = datt_ref[:, at : at + LANES]
        probs = across.probs(query, keyed)
        att_ref[:, at : at + LANES] = across.attend(probs, valued)
        for piece, pulled in enumerate(across.pull(probs, query, keyed, valued, grad)):
            dqkv_ref[:, piece * width + at : piece * width + at + LANES] = pulled
    for at in range(0, width, TILE):
        datt_ref[:, at : at + TILE] = nt(dqkv_ref[...], w_two[wide_rows(at), 0:wide]).astype(BF16)
    dy = cot + rms_pull(y_first, inv, datt_ref[...].astype(F32)).astype(BF16)
    dy_ref[...] = dy
    for at in range(0, width, TILE):
        back_grad = nn(dy, w_back[wide : wide + width, wide_rows(at)]).astype(BF16)
        g_send[:, :, at : at + TILE] = back_grad.reshape(groups, patches, TILE)
        pull.start(at // TILE)
    attended = att_ref[...]
    for at in range(0, width, TILE):
        out = y_first[:, at : at + TILE] + nn(attended, w_two[:, wide + at : wide + at + TILE])
        mixed_ref[:, :, at : at + TILE] = out.astype(BF16).reshape(groups, patches, TILE)

    def through(low, high, at):
        total = 0.0
        for piece in range(3):
            here = slice(piece * width + low, piece * width + high)
            total = total + nn(dqkv_ref[:, here], w_back[here, at : at + TILE])
        return total

    for block in range(width // LANES):
        at = block * LANES
        if at % TILE == 0:
            if at == TILE:
                for column in range(0, width, TILE):
                    sum_ref[:, column : column + TILE] = through(0, TILE, column)
            pull.wait(at // TILE)
            datt_ref[:, at : at + TILE] = g_recv[:, :, at : at + TILE].reshape(rows, TILE)
        query, keyed, valued = (part_at(qkv_ref, piece, at) for piece in range(3))
        probs = probs_ref[block * stacked : (block + 1) * stacked, :]
        grad = datt_ref[:, at : at + LANES]
        for piece, pulled in enumerate(space.pull(probs, query, keyed, valued, grad)):
            dqkv_ref[:, piece * width + at : piece * width + at + LANES] = pulled
    for at in range(0, width, TILE):
        grad = (sum_ref[:, at : at + TILE] + through(TILE, width, at)).astype(BF16)
        h_send[:, :, at : at + TILE] = grad.reshape(groups, patches, TILE)
    home.start()
    own = x_send[...].reshape(rows, width).astype(F32)
    inv, _ = rms_parts(own)
    for gather in (one, two):
        gather.drain()
    for tile in range(home.tiles):
        home.wait(tile)
    first = rms_pull(own, inv, h_recv[...].reshape(rows, width).astype(F32)).astype(BF16)
    grad_ref[...] = (dy_ref[...] + first).reshape(groups, patches, width)
    for exchange in (bands, back, pull, home):
        exchange.drain()


def wide_rows(at):
    return slice(at, at + TILE)


def local_bands(tokens, cotangent, w_sqkv, w_so, w_gqkv, w_go, keep):
    patches, groups, width = tokens.shape
    rows = patches * groups
    head = width // H
    count = lax.axis_size("grid")
    depth = w_sqkv.shape[0]
    banded = (groups, patches, width)
    flat, wide = (rows, width), (rows, 3 * width)
    full = (depth * count, 4 * width)
    shapes = [full, full, tokens.shape, tokens.shape]
    shapes += [banded] * 8
    shapes += [banded, flat, wide, wide, flat, flat, (4 * width, full[0])]
    anywhere = pl.BlockSpec(memory_space=pl.ANY)
    vmem = pl.BlockSpec(memory_space=pltpu.VMEM)
    product = 2 * rows * width * width
    mixed, grad = pl.pallas_call(
        partial(layer_kernel, head),
        in_specs=[anywhere] * 6 + [vmem],
        out_specs=(vmem, vmem),
        out_shape=(jax.ShapeDtypeStruct(banded, BF16),) * 2,
        scratch_shapes=[pltpu.VMEM(shape, BF16) for shape in shapes]
        + [pltpu.VMEM((H * rows, rows), F32), pltpu.VMEM(flat, F32)]
        + [pltpu.SemaphoreType.DMA((TRANSFERS + 32,)), pltpu.SemaphoreType.DMA((TRANSFERS,))] * 2
        + [pltpu.SemaphoreType.DMA((4, 2)), pltpu.SemaphoreType.DMA((4, 2)), pltpu.SemaphoreType.DMA((6,))]
        + [pltpu.SemaphoreType.REGULAR((6,))],
        compiler_params=pltpu.CompilerParams(
            collective_id=0, has_side_effects=True, vmem_limit_bytes=60 * 2**20
        ),
        cost_estimate=pl.CostEstimate(
            flops=21 * product, bytes_accessed=2**20, transcendentals=0
        ),
    )(tokens, cotangent, w_sqkv, w_so, w_gqkv, w_go, keep)
    return mixed.transpose(1, 0, 2), grad.transpose(1, 0, 2)


def local(tokens, *rest):
    if lax.axis_size("grid") == tokens.shape[1]:
        return local_bands(tokens, *rest)
    return local_any(tokens, *rest)


def solution(mesh):
    placed = (
        P(("parts", "grid"), None, None),
        P(("parts", "grid"), None, None),
        P("grid", None),
        P("grid", None),
        P("grid", None),
        P("grid", None),
        P(None, "parts"),
    )
    return jax.shard_map(
        local,
        mesh=mesh,
        in_specs=placed,
        out_specs=(P(("parts", "grid"), None, None), P(("parts", "grid"), None, None)),
        check_vma=False,
    )
```

```python
from functools import partial

import jax
import jax.numpy as jnp
from jax import lax
from jax.experimental import pallas as pl
from jax.experimental.pallas import tpu as pltpu
from jax.sharding import PartitionSpec as P

H = 16
G = 32


def rms_normalize(values):
    wide = values.astype(jnp.float32)
    meansq = jnp.mean(wide * wide, axis=-1, keepdims=True)
    return (wide * lax.rsqrt(meansq + 1e-06)).astype(jnp.bfloat16)


def project_spatial(tokens, weight):
    patches, groups, width = tokens.shape
    normed = rms_normalize(tokens).reshape(patches * groups, width)
    stacked = jnp.dot(normed, weight, preferred_element_type=jnp.float32).astype(jnp.bfloat16)
    stacked = stacked.reshape(patches, groups, 3, width).transpose(2, 0, 1, 3)
    return stacked.reshape(3, patches, groups * width)


def pair_attention(operands):
    stacked, keep_row = operands
    query, keyed, valued = (stacked[0], stacked[1], stacked[2])
    scale = query.shape[-1] ** (-0.5)
    scores = jnp.dot(query, keyed.T, preferred_element_type=jnp.float32) * scale
    weights = jnp.exp(scores) * keep_row[None, :]
    probs = (weights / jnp.sum(weights, axis=-1, keepdims=True)).astype(jnp.bfloat16)
    return jnp.dot(probs, valued, preferred_element_type=jnp.float32).astype(jnp.bfloat16)


def spatial_attention(stacked, keep_rows, attend):
    three, patches, columns = stacked.shape
    pairs = keep_rows.shape[0]
    split = stacked.reshape(3, patches, pairs, columns // pairs).transpose(2, 0, 1, 3)
    result = lax.map(attend, (split, keep_rows))
    return result.transpose(1, 0, 2).reshape(patches, columns)


def block_group(tokens, attended, w_so, w_gqkv, w_go):
    patches, groups, width = tokens.shape
    rows = patches * groups
    heads = H
    y_first = (
        tokens.reshape(rows, width).astype(jnp.float32)
        + jnp.dot(attended.reshape(rows, width), w_so, preferred_element_type=jnp.float32)
    ).astype(jnp.bfloat16)
    normed = rms_normalize(y_first)
    stacked = jnp.dot(normed, w_gqkv, preferred_element_type=jnp.float32).astype(jnp.bfloat16)
    stacked = stacked.reshape(patches, groups, 3, heads, width // heads)
    query = stacked[:, :, 0].astype(jnp.float32)
    keyed = stacked[:, :, 1].astype(jnp.float32)
    valued = stacked[:, :, 2].astype(jnp.float32)
    scale = (width // heads) ** (-0.5)
    scores = jnp.einsum("pgne,pkne->pngk", query, keyed) * scale
    weights = jnp.exp(scores)
    probs = (weights / jnp.sum(weights, axis=-1, keepdims=True)).astype(jnp.bfloat16)
    result = jnp.einsum("pngk,pkne->pgne", probs.astype(jnp.float32), valued).astype(jnp.bfloat16)
    result = result.reshape(rows, width)
    mixed = (
        y_first.astype(jnp.float32) + jnp.dot(result, w_go, preferred_element_type=jnp.float32)
    ).astype(jnp.bfloat16)
    return mixed.reshape(patches, groups, width)


def local_any(tokens, cotangent, w_sqkv, w_so, w_gqkv, w_go, keep):
    grid_size = lax.axis_size("grid")
    position = lax.axis_index("grid")
    full_sqkv, full_so, full_gqkv, full_go = (
        lax.all_gather(w_sqkv, "grid", axis=0, tiled=True),
        lax.all_gather(w_so, "grid", axis=0, tiled=True),
        lax.all_gather(w_gqkv, "grid", axis=0, tiled=True),
        lax.all_gather(w_go, "grid", axis=0, tiled=True),
    )
    stacked, pull_first = jax.vjp(partial(project_spatial, weight=full_sqkv), tokens)
    banded = lax.all_to_all(stacked, "grid", split_axis=2, concat_axis=1, tiled=True)
    pairs = G * H // grid_size
    pair_ids = position * pairs + jnp.arange(pairs, dtype=jnp.int32)
    select = (pair_ids[:, None] // H == jnp.arange(G, dtype=jnp.int32)[None, :]).astype(jnp.float32)
    keep_rows = jnp.dot(select, keep.astype(jnp.float32), precision=lax.Precision.HIGHEST)
    attend = jax.checkpoint(pair_attention)
    attended_bands, pull_spatial = jax.vjp(
        partial(spatial_attention, keep_rows=keep_rows, attend=attend), banded
    )
    attended = lax.all_to_all(attended_bands, "grid", split_axis=0, concat_axis=1, tiled=True)
    mixed, pull_group = jax.vjp(
        partial(block_group, w_so=full_so, w_gqkv=full_gqkv, w_go=full_go), tokens, attended
    )
    grad_direct, grad_attended = pull_group(cotangent)
    grad_bands = lax.all_to_all(grad_attended, "grid", split_axis=1, concat_axis=0, tiled=True)
    (grad_banded,) = pull_spatial(grad_bands)
    grad_stacked = lax.all_to_all(grad_banded, "grid", split_axis=1, concat_axis=2, tiled=True)
    (grad_first,) = pull_first(grad_stacked)
    return (mixed, grad_direct + grad_first)

F32 = jnp.float32
BF16 = jnp.bfloat16
LANES = 128
EPS = 1e-06
TILE = 512
SPLIT = (2, 2, 2)
TRANSFERS = 93
LAG = 12
PUMP_FROM = 12
PUMP_EVERY = 1
PUMP_BLOCK = 0
PUMP_TURN = 1
MESH = pl.DeviceIdType.MESH


def nn(a, b):
    return lax.dot_general(a, b, (((1,), (0,)), ((), ())), preferred_element_type=F32)


def nt(a, b):
    return lax.dot_general(a, b, (((1,), (1,)), ((), ())), preferred_element_type=F32)


def tn(a, b):
    return lax.dot_general(a, b, (((0,), (0,)), ((), ())), preferred_element_type=F32)


def rms_parts(wide):
    inv = lax.rsqrt(jnp.mean(wide * wide, axis=-1, keepdims=True) + EPS)
    return inv, (wide * inv).astype(BF16)


def rms_pull(wide, inv, grad):
    inner = jnp.mean(grad * wide, axis=-1, keepdims=True)
    return grad * inv - wide * (inv * inv * inv * inner)


class Heads:
    def __init__(self, head, rows, mask):
        lane = lax.broadcasted_iota(jnp.int32, (1, LANES), 1)
        self.count = LANES // head
        self.rows = rows
        scale = head ** (-0.5)
        plain = [(lane // head == index).astype(F32) for index in range(self.count)]
        self.plain = [one.astype(BF16) for one in plain]
        self.scaled = [(one * scale).astype(BF16) for one in plain]
        self.mask = jnp.concatenate([mask] * self.count, axis=0)

    def stack(self, block, selects):
        return jnp.concatenate([block * select for select in selects], axis=0)

    def beside(self, stacked):
        rows = self.rows
        return jnp.concatenate(
            [stacked[at * rows : (at + 1) * rows] for at in range(self.count)], axis=1
        )

    def probs(self, query, keyed):
        scores = nt(self.stack(query, self.scaled), keyed)
        weights = jnp.where(self.mask, jnp.exp(scores), 0.0)
        return weights * (1.0 / jnp.sum(weights, axis=-1, keepdims=True))

    def attend(self, probs, valued):
        return nn(self.beside(probs.astype(BF16)), self.stack(valued, self.plain)).astype(BF16)

    def pull(self, probs, query, keyed, valued, grad):
        grads = self.stack(grad, self.plain)
        dprobs = nt(grads, valued).astype(BF16).astype(F32)
        inner = jnp.sum(dprobs * probs, axis=-1, keepdims=True)
        dscores = (probs * (dprobs - inner)).astype(BF16)
        dquery = nn(self.beside(dscores), self.stack(keyed, self.scaled))
        dkeyed = tn(dscores, self.stack(query, self.scaled))
        dvalued = tn(probs.astype(BF16), grads)
        return dquery.astype(BF16), dkeyed.astype(BF16), dvalued.astype(BF16)


def part_cuts(columns):
    unit = columns // 32
    return ((0, 13 * unit), (13 * unit, 26 * unit), (26 * unit, columns))


class Gather:
    def __init__(self, full_ref, rows, send_sems, recv_sems):
        self.full, self.rows = full_ref, rows
        self.send_sems, self.recv_sems = send_sems, recv_sems
        self.cuts = part_cuts(full_ref.shape[1])
        self.part, self.me = lax.axis_index("parts"), lax.axis_index("grid")
        me = self.me
        self.core, self.x, self.y, self.z = me % 2, (me // 2) % 2, (me // 4) % 2, me // 8
        z = self.z
        self.origins = (z, z + 1 - 2 * (z % 2), 2 - z // 2, 3 * (1 - z // 2))
        self.inner = (z + 1) // 2 == 1
        self.outward = self.place(z + 1 - 2 * (z % 2))
        self.inward = self.place(3 - z)
        self.xp, self.yp = self.place(z, x=1), self.place(z, y=1)
        self.cp = self.place(z, core=1)
        self.sends, self.recvs = {}, {}
        self.sent, self.sent_inner = [], []

    def place(self, z, y=0, x=0, core=0):
        ny, nx, nc = SPLIT
        y = 1 - self.y if y else self.y
        x = 1 - self.x if x else self.x
        core = 1 - self.core if core else self.core
        return ((z * ny + y) * nx + x) * nc + core

    def region(self, piece, owner):
        low, high = self.cuts[piece]
        rows = self.rows
        return self.full.at[pl.ds(pl.multiple_of(owner * rows, rows), rows), low:high]

    def copy(self, name, way, piece, owner, peer):
        at = self.sends.setdefault((name, way), len(self.sends))
        got = self.recvs.setdefault(name, len(self.recvs))
        return pltpu.make_async_remote_copy(
            src_ref=self.region(piece, owner),
            dst_ref=self.region(piece, owner),
            send_sem=self.send_sems.at[at],
            recv_sem=self.recv_sems.at[got],
            device_id=(self.part, peer),
            device_id_type=MESH,
        )

    def send(self, name, piece, owner, peer):
        made = self.copy(name, 0, piece, owner, peer)
        made.start()
        self.sent.append(made)

    def send_inner(self, name, way, piece, owner, peer):
        made = self.copy(name, way, piece, owner, peer)
        pl.when(self.inner)(made.start)
        self.sent_inner.append(made)

    def arrive(self, name, piece, owner):
        got = self.recvs.setdefault(name, len(self.recvs))
        region = self.region(piece, owner)
        pltpu.make_async_remote_copy(
            src_ref=region,
            dst_ref=region,
            send_sem=self.send_sems.at[0],
            recv_sem=self.recv_sems.at[got],
            device_id=(self.part, self.xp),
            device_id_type=MESH,
        ).wait_recv()

    def owner(self, half, j, first, second):
        cross_y, cross_x = (first, second) if half == 0 else (second, first)
        return self.place(self.origins[j], y=cross_y, x=cross_x)

    def peers(self, half):
        return (self.yp, self.xp) if half == 0 else (self.xp, self.yp)

    def z_own(self, tag, piece, owner):
        self.send((tag, 1), piece, owner, self.outward)
        self.send_inner((tag, 2), 1, piece, owner, self.inward)

    def z_pass(self, tag, piece, owner, j):
        if j == 1:
            self.send_inner((tag, 3), 1, piece, owner, self.inward)
        else:
            self.send_inner((tag, j), 2, piece, owner, self.outward)

    def spread_line(self, half, j):
        mine = self.owner(half, j, 0, 0)
        if j:
            self.arrive((("z", half), j), half, mine)
            self.z_pass(("z", half), half, mine, j)
        self.send(("first", half, j), half, mine, self.peers(half)[0])
        self.send(("second", half, j, 0), half, mine, self.peers(half)[1])
        self.send(("core", half, j, 0, 0), half, mine, self.cp)

    def spread_first(self, half, j):
        got = self.owner(half, j, 1, 0)
        self.arrive(("first", half, j), half, got)
        self.send(("second", half, j, 1), half, got, self.peers(half)[1])
        self.send(("core", half, j, 1, 0), half, got, self.cp)

    def spread_second(self, half, j, first):
        got = self.owner(half, j, first, 1)
        self.arrive(("second", half, j, first), half, got)
        self.send(("core", half, j, first, 1), half, got, self.cp)

    def flat_owner(self, j, y, x):
        return self.place(self.origins[j], y=y, x=x)

    def flat_x(self):
        got = self.flat_owner(0, 0, 1)
        self.arrive(("flat x",), 2, got)
        self.send(("flat y", 1), 2, got, self.yp)
        self.z_own(("flat z", 0, 1), 2, got)
        self.send(("flat core", 0, 0, 1), 2, got, self.cp)

    def flat_y(self, x):
        got = self.flat_owner(0, 1, x)
        self.arrive(("flat y", x), 2, got)
        self.z_own(("flat z", 1, x), 2, got)
        self.send(("flat core", 0, 1, x), 2, got, self.cp)

    def flat_z(self, j, y, x):
        got = self.flat_owner(j, y, x)
        tag = ("flat z", y, x)
        self.arrive((tag, j), 2, got)
        self.z_pass(tag, 2, got, j)
        self.send(("flat core", j, y, x), 2, got, self.cp)

    def start(self):
        me = self.me
        for half in range(2):
            self.z_own(("z", half), half, me)
        self.send(("flat x",), 2, me, self.xp)
        for half in range(2):
            self.spread_line(half, 0)
        self.send(("flat y", 0), 2, me, self.yp)
        self.z_own(("flat z", 0, 0), 2, me)
        self.send(("flat core", 0, 0, 0), 2, me, self.cp)

    def steps(self):
        halves = range(2)
        plane = [(0, 0), (0, 1), (1, 0), (1, 1)]
        work = [partial(self.flat_x)]
        work += [partial(self.spread_first, half, 0) for half in halves]
        work += [partial(self.flat_y, x) for x in range(2)]
        for j in range(1, 4):
            work += [partial(self.spread_line, half, j) for half in halves]
            work += [partial(self.spread_second, half, j - 1, 0) for half in halves]
            work += [partial(self.spread_second, half, j - 1, 1) for half in halves]
            work += [partial(self.spread_first, half, j) for half in halves]
            work += [partial(self.flat_z, j, y, x) for y, x in plane]
        work += [partial(self.spread_second, half, 3, 0) for half in halves]
        work += [partial(self.spread_second, half, 3, 1) for half in halves]
        return work

    def finish(self):
        for j in range(4):
            for first in range(2):
                for second in range(2):
                    for half in range(2):
                        cross_y, cross_x = (first, second) if half == 0 else (second, first)
                        got = self.place(self.origins[j], y=cross_y, x=cross_x, core=1)
                        self.arrive(("core", half, j, first, second), half, got)
                    got = self.place(self.origins[j], y=first, x=second, core=1)
                    self.arrive(("flat core", j, first, second), 2, got)

    def drain(self):
        for made in self.sent:
            made.wait_send()

        @pl.when(self.inner)
        def _():
            for made in self.sent_inner:
                made.wait_send()


def flipped(me, bits, count):
    peer, unit = 0, 1
    while unit < count:
        mine, flip = (me // unit) % 2, (bits // unit) % 2
        peer = peer + unit * (mine + flip - 2 * mine * flip)
        unit *= 2
    return peer


class Exchange:
    def __init__(self, src, dst, send_sems, recv_sems, tiles=1):
        self.src, self.dst, self.send_sems, self.recv_sems = src, dst, send_sems, recv_sems
        self.part, self.me = lax.axis_index("parts"), lax.axis_index("grid")
        self.count, self.tiles = src.shape[0], tiles
        self.wide = src.shape[2] // tiles

    def columns(self, tile):
        return slice(tile * self.wide, (tile + 1) * self.wide)

    def start(self, tile=0):
        me, count, columns = self.me, self.count, self.columns(tile)

        def one(step, carry):
            peer = flipped(me, count - step, count)
            pltpu.make_async_remote_copy(
                src_ref=self.src.at[peer, :, columns],
                dst_ref=self.dst.at[me, :, columns],
                send_sem=self.send_sems.at[tile],
                recv_sem=self.recv_sems.at[tile],
                device_id=(self.part, peer),
                device_id_type=MESH,
            ).start()
            return carry

        lax.fori_loop(1, count, one, 0)
        self.dst[pl.ds(me, 1), :, columns] = self.src[pl.ds(me, 1), :, columns]

    def whole(self, tile):
        most, columns = self.count - 1, self.columns(tile)
        return pltpu.make_async_remote_copy(
            src_ref=self.src.at[0:most, :, columns],
            dst_ref=self.dst.at[0:most, :, columns],
            send_sem=self.send_sems.at[tile],
            recv_sem=self.recv_sems.at[tile],
            device_id=(self.part, (self.me + 1) % self.count),
            device_id_type=MESH,
        )

    def wait(self, tile=0):
        self.whole(tile).wait_recv()

    def drain(self):
        for tile in range(self.tiles):
            self.whole(tile).wait_send()


class Greeting:
    def __init__(self, gather, sems):
        self.at, self.sems = gather, sems

    def signal(self, sem, peer):
        pl.semaphore_signal(
            sem, inc=1, device_id=(self.at.part, peer), device_id_type=MESH
        )

    def neighbours(self):
        at, barrier = self.at, pltpu.get_barrier_semaphore()
        for peer in (at.xp, at.yp, at.cp, at.outward):
            self.signal(barrier, peer)

        @pl.when(at.inner)
        def _():
            self.signal(barrier, at.inward)

    def meet(self):
        at, barrier = self.at, pltpu.get_barrier_semaphore()
        pl.semaphore_wait(barrier, 4 + jnp.where(at.inner, 1, 0))
        self.signal(self.sems.at[0], at.cp)

    def stages(self):
        at, sems = self.at, self.sems
        order = (at.cp, at.xp, at.yp, at.outward)

        def pass_on(stage):
            pl.semaphore_wait(sems.at[stage], 1)
            self.signal(sems.at[stage + 1], order[stage + 1])

        def across():
            pl.semaphore_wait(sems.at[3], 1)

            @pl.when(at.inner)
            def _():
                self.signal(sems.at[4], at.inward)

        def ends():
            @pl.when(at.inner)
            def _():
                pl.semaphore_wait(sems.at[4], 1)
                self.signal(sems.at[5], at.outward)

            @pl.when(jnp.logical_not(at.inner))
            def _():
                pl.semaphore_wait(sems.at[5], 1)

        return [partial(pass_on, stage) for stage in range(3)] + [across, ends]


def layer_kernel(
    head,
    tok_hbm, cot_hbm, sqkv_hbm, so_hbm, gqkv_hbm, go_hbm, keep_ref,
    mixed_ref, grad_ref,
    w_one, w_two, tok_ref, cot_ref,
    x_send, x_recv, y_send, y_recv, g_send, g_recv, h_send, h_recv,
    cot_mine, dy_ref, qkv_ref, dqkv_ref, att_ref, datt_ref, w_back, probs_ref, sum_ref,
    send_one, recv_one, send_two, recv_two, a2a_send, a2a_recv, own_sems, hello,
):
    count = lax.axis_size("grid")
    part, me = lax.axis_index("parts"), lax.axis_index("grid")
    patches, groups, width = tok_ref.shape
    rows = patches * groups
    wide = 3 * width
    depth = sqkv_hbm.shape[0]
    mine = pl.ds(pl.multiple_of(me * depth, depth), depth)
    loads = [
        pltpu.make_async_copy(source, target, own_sems.at[at])
        for at, (source, target) in enumerate((
            (sqkv_hbm, w_one.at[mine, 0:wide]),
            (so_hbm, w_one.at[mine, wide : wide + width]),
            (gqkv_hbm, w_two.at[mine, 0:wide]),
            (go_hbm, w_two.at[mine, wide : wide + width]),
            (tok_hbm, tok_ref),
            (cot_hbm, cot_ref),
        ))
    ]
    for load in loads:
        load.start()

    one = Gather(w_one, depth, send_one, recv_one)
    two = Gather(w_two, depth, send_two, recv_two)
    greeting = Greeting(one, hello)
    bands = Exchange(x_send, x_recv, a2a_send.at[0], a2a_recv.at[0])
    back = Exchange(y_send, y_recv, a2a_send.at[1], a2a_recv.at[1])
    pull = Exchange(g_send, g_recv, a2a_send.at[2], a2a_recv.at[2], width // TILE)
    home = Exchange(h_send, h_recv, a2a_send.at[3], a2a_recv.at[3])

    greeting.neighbours()
    for load in loads[:4]:
        load.wait()
    greeting.meet()
    one.start()
    loads[4].wait()
    for at in range(patches):
        x_send[:, at, :] = tok_ref[at]
    loads[5].wait()
    for at in range(patches):
        cot_mine[:, at, :] = cot_ref[at]
    stages = greeting.stages()
    ahead = two.steps()

    def pump(steps):
        for _ in range(min(steps, len(ahead))):
            ahead.pop(0)()

    for at, step in enumerate(one.steps()):
        if at < len(stages):
            stages[at]()
        step()
        if at == len(stages):
            bands.start()
        if at == LAG:
            two.start()
        if at > PUMP_FROM and at % PUMP_EVERY == 0:
            pump(1)
    bands.wait()

    def part_at(ref, piece, at):
        return ref[:, piece * width + at : piece * width + at + LANES]

    x = x_recv[...].reshape(rows, width).astype(F32)
    _, normed = rms_parts(x)
    att_ref[...] = normed
    one.finish()
    normed = att_ref[...]
    for at in range(0, wide, TILE):
        qkv_ref[:, at : at + TILE] = nn(normed, w_one[:, at : at + TILE]).astype(BF16)
    pump(PUMP_BLOCK)
    keep_row = keep_ref[pl.ds(me, 1), :]
    space = Heads(head, rows, jnp.broadcast_to(keep_row, (rows, rows)) > 0)
    stacked = space.count * rows
    for block in range(width // LANES):
        at = block * LANES
        query, keyed, valued = (part_at(qkv_ref, piece, at) for piece in range(3))
        probs = space.probs(query, keyed)
        probs_ref[block * stacked : (block + 1) * stacked, :] = probs
        att_ref[:, at : at + LANES] = space.attend(probs, valued)
        pump(PUMP_BLOCK)
    attended = att_ref[...]
    for at in range(0, width, TILE):
        y = x[:, at : at + TILE] + nn(attended, w_one[:, wide + at : wide + at + TILE])
        y_send[:, :, at : at + TILE] = y.astype(BF16).reshape(groups, patches, TILE)
    back.start()
    for at in range(0, wide + width, LANES):
        w_back[at : at + LANES, :] = w_one[:, at : at + LANES].T
        if at % TILE == 0:
            pump(PUMP_TURN)
    pump(len(ahead))
    two.finish()

    cot = cot_mine[...].reshape(rows, width)
    for at in range(0, width, TILE):
        datt_ref[:, at : at + TILE] = nt(cot, w_two[wide_rows(at), wide : wide + width]).astype(BF16)
    back.wait()
    y_first = y_recv[...].reshape(rows, width).astype(F32)
    inv, normed = rms_parts(y_first)
    for at in range(0, wide, TILE):
        dqkv_ref[:, at : at + TILE] = nn(normed, w_two[:, at : at + TILE]).astype(BF16)
    row = lax.broadcasted_iota(jnp.int32, (rows, rows), 0)
    col = lax.broadcasted_iota(jnp.int32, (rows, rows), 1)
    across = Heads(head, rows, row % patches == col % patches)
    for block in range(width // LANES):
        at = block * LANES
        query, keyed, valued = (part_at(dqkv_ref, piece, at) for piece in range(3))
        grad = datt_ref[:, at : at + LANES]
        probs = across.probs(query, keyed)
        att_ref[:, at : at + LANES] = across.attend(probs, valued)
        for piece, pulled in enumerate(across.pull(probs, query, keyed, valued, grad)):
            dqkv_ref[:, piece * width + at : piece * width + at + LANES] = pulled
    for at in range(0, width, TILE):
        datt_ref[:, at : at + TILE] = nt(w_two[wide_rows(at), 0:wide], dqkv_ref[...]).T.astype(BF16)
    dy = cot + rms_pull(y_first, inv, datt_ref[...].astype(F32)).astype(BF16)
    dy_ref[...] = dy
    for at in range(0, width, TILE):
        back_grad = nn(dy, w_back[wide : wide + width, wide_rows(at)]).astype(BF16)
        g_send[:, :, at : at + TILE] = back_grad.reshape(groups, patches, TILE)
        pull.start(at // TILE)
    attended = att_ref[...]
    for at in range(0, width, TILE):
        out = y_first[:, at : at + TILE] + nn(attended, w_two[:, wide + at : wide + at + TILE])
        mixed_ref[:, :, at : at + TILE] = out.astype(BF16).reshape(groups, patches, TILE)

    def through(low, high, at):
        total = 0.0
        for piece in range(3):
            here = slice(piece * width + low, piece * width + high)
            total = total + nn(dqkv_ref[:, here], w_back[here, at : at + TILE])
        return total

    for block in range(width // LANES):
        at = block * LANES
        if at % TILE == 0:
            if at == TILE:
                for column in range(0, width, TILE):
                    sum_ref[:, column : column + TILE] = through(0, TILE, column)
            pull.wait(at // TILE)
            datt_ref[:, at : at + TILE] = g_recv[:, :, at : at + TILE].reshape(rows, TILE)
        query, keyed, valued = (part_at(qkv_ref, piece, at) for piece in range(3))
        probs = probs_ref[block * stacked : (block + 1) * stacked, :]
        grad = datt_ref[:, at : at + LANES]
        for piece, pulled in enumerate(space.pull(probs, query, keyed, valued, grad)):
            dqkv_ref[:, piece * width + at : piece * width + at + LANES] = pulled
    for at in range(0, width, TILE):
        grad = (sum_ref[:, at : at + TILE] + through(TILE, width, at)).astype(BF16)
        h_send[:, :, at : at + TILE] = grad.reshape(groups, patches, TILE)
    home.start()
    own = x_send[...].reshape(rows, width).astype(F32)
    inv, _ = rms_parts(own)
    for gather in (one, two):
        gather.drain()
    for tile in range(home.tiles):
        home.wait(tile)
    first = rms_pull(own, inv, h_recv[...].reshape(rows, width).astype(F32)).astype(BF16)
    grad_ref[...] = (dy_ref[...] + first).reshape(groups, patches, width)
    for exchange in (bands, back, pull, home):
        exchange.drain()


def wide_rows(at):
    return slice(at, at + TILE)


def local_bands(tokens, cotangent, w_sqkv, w_so, w_gqkv, w_go, keep):
    patches, groups, width = tokens.shape
    rows = patches * groups
    head = width // H
    count = lax.axis_size("grid")
    depth = w_sqkv.shape[0]
    banded = (groups, patches, width)
    flat, wide = (rows, width), (rows, 3 * width)
    full = (depth * count, 4 * width)
    shapes = [full, full, tokens.shape, tokens.shape]
    shapes += [banded] * 8
    shapes += [banded, flat, wide, wide, flat, flat, (4 * width, full[0])]
    anywhere = pl.BlockSpec(memory_space=pl.ANY)
    vmem = pl.BlockSpec(memory_space=pltpu.VMEM)
    product = 2 * rows * width * width
    mixed, grad = pl.pallas_call(
        partial(layer_kernel, head),
        in_specs=[anywhere] * 6 + [vmem],
        out_specs=(vmem, vmem),
        out_shape=(jax.ShapeDtypeStruct(banded, BF16),) * 2,
        scratch_shapes=[pltpu.VMEM(shape, BF16) for shape in shapes]
        + [pltpu.VMEM((H * rows, rows), F32), pltpu.VMEM(flat, F32)]
        + [pltpu.SemaphoreType.DMA((TRANSFERS + 32,)), pltpu.SemaphoreType.DMA((TRANSFERS,))] * 2
        + [pltpu.SemaphoreType.DMA((4, 2)), pltpu.SemaphoreType.DMA((4, 2)), pltpu.SemaphoreType.DMA((6,))]
        + [pltpu.SemaphoreType.REGULAR((6,))],
        compiler_params=pltpu.CompilerParams(
            collective_id=0, has_side_effects=True, vmem_limit_bytes=60 * 2**20
        ),
        cost_estimate=pl.CostEstimate(
            flops=21 * product, bytes_accessed=2**20, transcendentals=0
        ),
    )(tokens, cotangent, w_sqkv, w_so, w_gqkv, w_go, keep)
    return mixed.transpose(1, 0, 2), grad.transpose(1, 0, 2)


def local(tokens, *rest):
    if lax.axis_size("grid") == tokens.shape[1]:
        return local_bands(tokens, *rest)
    return local_any(tokens, *rest)


def solution(mesh):
    placed = (
        P(("parts", "grid"), None, None),
        P(("parts", "grid"), None, None),
        P("grid", None),
        P("grid", None),
        P("grid", None),
        P("grid", None),
        P(None, "parts"),
    )
    return jax.shard_map(
        local,
        mesh=mesh,
        in_specs=placed,
        out_specs=(P(("parts", "grid"), None, None), P(("parts", "grid"), None, None)),
        check_vma=False,
    )
```
